32 devices in a mesh: dp: 4 (over z), row: 4 (over x, core), col: 2 (over y).
Axes of the slice: x: 2, y: 2, z: 4, core: 2. Of those that a mesh axis runs over, the one named last changes fastest.
Arguments:
- layer_input: bfloat16 [8, 512, 2048], P('dp', 'row'), may hold values from -12 to 12, as said below
- cotangent: bfloat16 [8, 512, 2048], P('dp', 'row'), may hold values from -6 to 6
- lengths: int32 [8], replicated, may hold values from 128 to 512, as said below
- deal_slot: int32 [8], replicated, may hold values from 0 to 7, as said below
- query_weight: bfloat16 [2048, 2048], P('row', 'col'), may hold values from -0.125 to 0.125
- key_weight: bfloat16 [2048, 2048], P('row', 'col'), may hold values from -0.125 to 0.125
- value_weight: bfloat16 [2048, 2048], P('row', 'col'), may hold values from -0.125 to 0.125
- out_weight: bfloat16 [2048, 2048], P('col', 'row'), may hold values from -0.125 to 0.125
- query_gain: bfloat16 [2048], P('col'), may hold values from 0.5 to 1.5
- key_gain: bfloat16 [2048], P('col'), may hold values from 0.5 to 1.5
- attn_gain: bfloat16 [2048], P('row'), may hold values from 0.5 to 1.5
- gate_weight: bfloat16 [2048, 8192], P('row', 'col'), may hold values from -0.125 to 0.125
- up_weight: bfloat16 [2048, 8192], P('row', 'col'), may hold values from -0.125 to 0.125
- down_weight: bfloat16 [8192, 2048], P('col', 'row'), may hold values from -0.0625 to 0.0625
- mlp_gain: bfloat16 [2048], P('row'), may hold values from 0.5 to 1.5
Outputs:
- output: bfloat16 [8, 512, 2048], P('dp', 'row')
- grad_input: bfloat16 [8, 512, 2048], P('dp', 'row')
- grad_query: float32 [2048, 2048], P('row', 'col')
- grad_key: float32 [2048, 2048], P('row', 'col')
- grad_value: float32 [2048, 2048], P('row', 'col')
- grad_out: float32 [2048, 2048], P('col', 'row')
- grad_query_gain: float32 [2048], P('col')
- grad_key_gain: float32 [2048], P('col')
- grad_attn_gain: float32 [2048], P('row')
- grad_gate: float32 [2048, 8192], P('row', 'col')
- grad_up: float32 [2048, 8192], P('row', 'col')
- grad_down: float32 [8192, 2048], P('col', 'row')
- grad_mlp_gain: float32 [2048], P('row')
- rms_stats: float32 [4, 3], replicated
The draws below stay inside these ranges and needn't reach their ends.
Inputs may be any that keep to these rules, and one draw needn't show every extreme that they name: `layer_input`: activations; each sequence has its own scale. `lengths`: some sequence has 512 valid tokens and some 512 // 4. A permutation of the 8 slots; sequence i goes to position deal_slot[i] % 2 of group deal_slot[i] // 2; the 2 sequences held by one group, sequences i with i // 2 equal, go to 2 different groups.
All inputs are finite; a program needn't handle non-finite values.
Results may differ from the reference program's by a relative error of at most 0.023.
Values may be sent and summed in bfloat16 or wider, within the bound.
No kernel may reach another device: no remote copies, remote signals or barrier semaphores. Data moves between devices by JAX's collectives and lax.ppermute only.
A program may use at most 512 MiB of HBM per device.

```python
import math
import jax
import jax.numpy as jnp
from jax import lax

D = 2048
HEADS = 16
HD = 128
FF = 8192
SEQ_LEN = 512
GROUPS = 4
SEQ_GRP = 2
NSEQ = 8


def draw_layer_input(key, part):
    scale_key, value_key = jax.random.split(key)
    factors = jnp.exp(jax.random.uniform(scale_key, (NSEQ, 1, 1), jnp.float32, math.log(0.5), math.log(2.0)))
    values = jnp.clip(jax.random.normal(value_key, (NSEQ, SEQ_LEN, D), jnp.float32), -6.0, 6.0)
    return (values * factors).astype(jnp.bfloat16)


def draw_lengths(key, part):
    base_key, first_key, other_key = jax.random.split(key, 3)
    base_len = jax.random.randint(base_key, (NSEQ,), SEQ_LEN // 4, SEQ_LEN + 1)
    first_pick = jax.random.randint(first_key, (), 0, NSEQ)
    other_pick = (first_pick + jax.random.randint(other_key, (), 1, NSEQ)) % NSEQ
    base_len = base_len.at[first_pick].set(SEQ_LEN)
    base_len = base_len.at[other_pick].set(SEQ_LEN // 4)
    return base_len.astype(jnp.int32)


def draw_deal_slot(key, part):
    offset_key, source_key, target_key, class_key = jax.random.split(key, 4)
    offsets = jax.random.permutation(offset_key, GROUPS)[:SEQ_GRP]
    source_label = jax.random.permutation(source_key, GROUPS)
    target_label = jax.random.permutation(target_key, GROUPS)
    classes = jax.vmap(lambda one_key: jax.random.permutation(one_key, SEQ_GRP))(jax.random.split(class_key, GROUPS))
    group_ids = jnp.arange(GROUPS, dtype=jnp.int32)[:, None]
    targets = target_label[(source_label[group_ids] + offsets[classes]) % GROUPS]
    return (targets * SEQ_GRP + classes).reshape(-1).astype(jnp.int32)


def block_scale(rng, dims, shards, low, high):
    gain, own = 1.0, jax.random.fold_in(rng, 6)
    for axis_at, parts in shards:
        heights = jnp.exp(jax.random.uniform(jax.random.fold_in(own, axis_at), (parts,), jnp.float32, low / len(shards), high / len(shards)))
        gain = gain * jnp.repeat(heights, dims[axis_at] // parts).reshape([-1 if axis == axis_at else 1 for axis in range(len(dims))])
    return gain


def bell_draw(own_key, shape, scale, reach, pieces=(), kind=jnp.bfloat16):
    drawn = scale * jax.random.normal(own_key, shape, jnp.float32)
    if pieces:
        drawn = drawn * block_scale(own_key, shape, pieces, -0.22, 0.18)
    return jnp.clip(drawn, -reach, reach).astype(kind)


def setup_inputs(seed: int = 0) -> dict:
    splits = jax.random.split(jax.random.key(seed), 16)
    layer_input = draw_layer_input(jax.random.fold_in(splits[15], 71), 0)
    cotangent = bell_draw(splits[1], (NSEQ, SEQ_LEN, D), 1.0, 6.0, ((0, 4), (1, 4)))
    lengths = draw_lengths(jax.random.fold_in(splits[15], 71), 0)
    deal_slot = draw_deal_slot(jax.random.fold_in(splits[15], 71), 0)
    query_weight = bell_draw(splits[4], (D, D), D ** -0.5, 0.125, ((0, 4), (1, 2)))
    key_weight = bell_draw(splits[5], (D, D), D ** -0.5, 0.125, ((0, 4), (1, 2)))
    value_weight = bell_draw(splits[6], (D, D), D ** -0.5, 0.125, ((0, 4), (1, 2)))
    out_weight = bell_draw(splits[7], (D, D), D ** -0.5, 0.125, ((0, 2), (1, 4)))
    query_gain = jnp.clip(1.0 + 0.1 * jax.random.normal(splits[8], (D,), jnp.float32), 0.5, 1.5).astype(jnp.bfloat16)
    key_gain = jnp.clip(1.0 + 0.1 * jax.random.normal(splits[9], (D,), jnp.float32), 0.5, 1.5).astype(jnp.bfloat16)
    attn_gain = jnp.clip(1.0 + 0.1 * jax.random.normal(splits[10], (D,), jnp.float32), 0.5, 1.5).astype(jnp.bfloat16)
    gate_weight = bell_draw(splits[11], (D, FF), D ** -0.5, 0.125, ((0, 4), (1, 2)))
    up_weight = bell_draw(splits[12], (D, FF), D ** -0.5, 0.125, ((0, 4), (1, 2)))
    down_weight = bell_draw(splits[13], (FF, D), FF ** -0.5, 0.0625, ((0, 2), (1, 4)))
    mlp_gain = jnp.clip(1.0 + 0.1 * jax.random.normal(splits[14], (D,), jnp.float32), 0.5, 1.5).astype(jnp.bfloat16)
    return {"layer_input": layer_input, "cotangent": cotangent, "lengths": lengths, "deal_slot": deal_slot, "query_weight": query_weight, "key_weight": key_weight, "value_weight": value_weight, "out_weight": out_weight, "query_gain": query_gain, "key_gain": key_gain, "attn_gain": attn_gain, "gate_weight": gate_weight, "up_weight": up_weight, "down_weight": down_weight, "mlp_gain": mlp_gain}


EPSILON = 1e-06
ROPE_THETA = 500000.0
MASK_VALUE = 1e+30

@jax.custom_vjp
def low(v):
    return lax.optimization_barrier(v.astype(jnp.bfloat16)).astype(jnp.float32)

@jax.custom_vjp
def low_back(v):
    return v

def low_keep(v):
    return (low(v), None)

def low_pass(kept, grad):
    return (grad,)

def back_keep(v):
    return (v, None)

def back_low(kept, grad):
    return (low(grad),)
low.defvjp(low_keep, low_pass)
low_back.defvjp(back_keep, back_low)

def rms_scale(matrix):
    return lax.rsqrt(lax.optimization_barrier(jnp.mean(matrix * matrix, axis=-1, keepdims=True)) + EPSILON)

def rotate_pairs(matrix, cos_table, sin_table):
    half_size = matrix.shape[-1] // 2
    first_half = matrix[..., :half_size]
    second_half = matrix[..., half_size:]
    return jnp.concatenate([first_half * cos_table - second_half * sin_table, second_half * cos_table + first_half * sin_table], axis=-1)

def product(left_side, right_side):
    return jnp.dot(left_side, right_side, precision=lax.Precision.HIGHEST)

def one_sequence(params, tokens, length):
    query_weight, key_weight, value_weight, out_weight, query_gain, key_gain, attn_gain, gate_weight, up_weight, down_weight, mlp_gain = params
    places = jnp.arange(SEQ_LEN, dtype=jnp.int32)
    valid_rows = (places < length).astype(tokens.dtype)[:, None]
    inputs = tokens * valid_rows
    query_raw = low_back(product(inputs, query_weight))
    key_raw = low_back(product(inputs, key_weight))
    value_raw = low(low_back(product(inputs, value_weight)))
    q_normed = query_raw * rms_scale(query_raw) * query_gain
    k_normed = key_raw * rms_scale(key_raw) * key_gain
    frequency = ROPE_THETA ** (-(jnp.arange(HD // 2).astype(tokens.dtype) * 2.0 / HD))
    angles = places.astype(tokens.dtype)[:, None] * frequency[None, :]
    cos_table = jnp.cos(angles)[:, None, :]
    sin_table = jnp.sin(angles)[:, None, :]
    q_rot = low(rotate_pairs(q_normed.reshape(SEQ_LEN, HEADS, HD), cos_table, sin_table))
    k_rot = low(rotate_pairs(k_normed.reshape(SEQ_LEN, HEADS, HD), cos_table, sin_table))
    value_heads = value_raw.reshape(SEQ_LEN, HEADS, HD)
    raw_scores = jnp.einsum('qhd,khd->hqk', q_rot, k_rot, precision=lax.Precision.HIGHEST) * HD ** (-0.5)
    scores = low_back(raw_scores)
    allowed = (places[None, :] <= places[:, None]) & (places[None, :] < length)
    scores = jnp.where(allowed[None], scores, -MASK_VALUE)
    prob_low = low(jax.nn.softmax(scores, axis=-1))
    attn_mix = jnp.einsum('hqk,khd->qhd', prob_low, value_heads, precision=lax.Precision.HIGHEST).reshape(SEQ_LEN, D)
    attn_mix = low(low_back(attn_mix))
    attn_raw = low_back(product(attn_mix, out_weight))
    branch_a = attn_raw * rms_scale(attn_raw) * attn_gain
    hidden = inputs + branch_a
    hidden_low = low(hidden)
    gate_pre = low_back(product(hidden_low, gate_weight))
    up_pre = low_back(product(hidden_low, up_weight))
    inner_low = low(jax.nn.silu(gate_pre) * up_pre)
    mlp_raw = low_back(product(inner_low, down_weight))
    branch_m = mlp_raw * rms_scale(mlp_raw) * mlp_gain
    result = (hidden + branch_m) * valid_rows
    square_sums = jnp.stack([jnp.sum(result * result), jnp.sum(branch_a * branch_a * valid_rows), jnp.sum(branch_m * branch_m * valid_rows)])
    return (result, square_sums)

def make_layer(lengths):

    def layer(tokens, *params):

        def scan_step(scan_carry, scan_item):
            result, square_sums = jax.checkpoint(one_sequence)(params, scan_item[0], scan_item[1])
            return (scan_carry, (result, square_sums))
        carry_zero = jnp.zeros((), tokens.dtype)
        unused, outputs = lax.scan(scan_step, carry_zero, (tokens, lengths))
        return (outputs[0], outputs[1])
    return layer

def reference(layer_input, cotangent, lengths, deal_slot, query_weight, key_weight, value_weight, out_weight, query_gain, key_gain, attn_gain, gate_weight, up_weight, down_weight, mlp_gain):
    params = tuple((weight.astype(jnp.float32) for weight in (query_weight, key_weight, value_weight, out_weight, query_gain, key_gain, attn_gain, gate_weight, up_weight, down_weight, mlp_gain)))
    inputs = layer_input.astype(jnp.float32)
    result, pullback, square_sums = jax.vjp(make_layer(lengths), inputs, *params, has_aux=True)
    gradients = pullback(cotangent.astype(jnp.float32))
    member = ((deal_slot // SEQ_GRP)[:, None] == jnp.arange(GROUPS, dtype=jnp.int32)[None, :]).astype(jnp.float32)
    totals = jnp.dot(member.T, square_sums, precision=lax.Precision.HIGHEST)
    counts = jnp.dot(member.T, lengths.astype(jnp.float32), precision=lax.Precision.HIGHEST)
    rms_stats = jnp.sqrt(totals / (counts[:, None] * D))
    return (result.astype(jnp.bfloat16), gradients[0].astype(jnp.bfloat16), gradients[1], gradients[2], gradients[3], gradients[4], gradients[5], gradients[6], gradients[7], gradients[8], gradients[9], gradients[10], gradients[11], rms_stats)
```

```python
import jax
import jax.numpy as jnp
from jax import lax
from jax.sharding import PartitionSpec as P

HD = 128
EPSILON = 1e-06
ROPE_THETA = 500000.0
MASK_VALUE = 1e30
BF = jnp.bfloat16
F32 = jnp.float32


def rms_scale(matrix):
    return lax.rsqrt(jnp.mean(matrix * matrix, axis=-1, keepdims=True) + EPSILON)


def rotate_pairs(matrix, cos_table, sin_table):
    half_size = matrix.shape[-1] // 2
    first_half = matrix[..., :half_size]
    second_half = matrix[..., half_size:]
    return jnp.concatenate(
        [
            first_half * cos_table - second_half * sin_table,
            second_half * cos_table + first_half * sin_table,
        ],
        axis=-1,
    )


def dot(left_side, right_side):
    return jnp.dot(left_side, right_side, preferred_element_type=F32)


def against(left_side, right_side):
    return lax.dot_general(
        left_side, right_side, (((0,), (0,)), ((), ())), preferred_element_type=F32
    )


def through(left_side, weight):
    return lax.dot_general(
        left_side, weight, (((1,), (1,)), ((), ())), preferred_element_type=F32
    )


class Plane:
    def __init__(self, width):
        self.rows = lax.axis_size("row")
        self.cols = lax.axis_size("col")
        self.row = lax.axis_index("row")
        self.col = lax.axis_index("col")
        self.part = width // self.rows

    def hop(self, array, row_xor, col_xor=0):
        if row_xor and col_xor:
            pairs = [
                (a * self.cols + b, (a ^ row_xor) * self.cols + (b ^ col_xor))
                for a in range(self.rows)
                for b in range(self.cols)
            ]
            return lax.ppermute(array, ("row", "col"), pairs)
        if row_xor:
            return lax.ppermute(array, "row", [(a, a ^ row_xor) for a in range(self.rows)])
        if col_xor:
            return lax.ppermute(array, "col", [(a, a ^ col_xor) for a in range(self.cols)])
        return array

    def slot(self, array, index):
        return array[..., index * self.part : (index + 1) * self.part]

    def turn(self, array, row_xor):
        if row_xor == 0:
            return array
        return jnp.concatenate(
            [self.slot(array, index ^ row_xor) for index in range(self.rows)], axis=-1
        )

    def relative(self, array):
        return jnp.concatenate(
            [
                lax.dynamic_slice_in_dim(
                    array, (self.row ^ index) * self.part, self.part, axis=array.ndim - 1
                )
                for index in range(self.rows)
            ],
            axis=-1,
        )

    def gather(self, own):
        blocks = {(0, 0): own}
        if self.rows == 4 and self.cols == 2:
            half = own.shape[0] // 2
            blocks[0, 2] = self.hop(self.turn(own, 2), 2)
            blocks[1, 0] = self.hop(own, 0, 1)
            blocks[1, 2] = jnp.concatenate(
                [
                    self.hop(blocks[0, 2][:half], 0, 1),
                    self.hop(self.turn(blocks[1, 0][half:], 2), 2),
                ],
                axis=0,
            )
        else:
            for col_xor in reversed(range(self.cols)):
                for row_xor in reversed(range(0, self.rows, 2)):
                    blocks[col_xor, row_xor] = self.hop(self.turn(own, row_xor), row_xor, col_xor)
        return self.over_cores(blocks)

    def over_cores(self, blocks):
        for col_xor in range(self.cols):
            for row_xor in range(0, self.rows, 2):
                blocks[col_xor, row_xor + 1] = self.hop(
                    self.turn(blocks[col_xor, row_xor], 1), 1
                )
        return jnp.concatenate(
            [blocks[b, a] for b in range(self.cols) for a in range(self.rows)], axis=0
        )

    def gather_columns(self, own):
        blocks = {}
        for row_xor in range(0, self.rows, 2):
            arrived = self.hop(self.turn(own[0], row_xor), row_xor)
            for col_xor in range(self.cols):
                if row_xor:
                    blocks[col_xor, row_xor] = self.hop(arrived, 0, col_xor)
                else:
                    blocks[col_xor, row_xor] = own[col_xor]
        return self.over_cores(blocks)

    def scatter(self, partial):
        tokens = partial.shape[0] // (self.rows * self.cols)
        blocks = partial.reshape(self.cols, self.rows, tokens, -1)
        if self.rows == 4 and self.cols == 2:
            half = tokens // 2
            away = self.hop(self.turn(jnp.stack([blocks[:, 1], blocks[:, 3]]), 1), 1)
            near = [blocks[:, 2 * k].astype(F32) + away[k].astype(F32) for k in range(2)]
            by_row = self.hop(self.turn(near[1][:, :half].astype(BF), 2), 2).astype(F32)
            far = jnp.stack([near[0][1, half:], near[1][1, half:]]).astype(BF)
            by_col = self.hop(far, 0, 1).astype(F32)
            first = [near[0][k, :half] + by_row[k] for k in range(2)]
            second = [near[k][0, half:] + by_col[k] for k in range(2)]
            last_col = self.hop(first[1].astype(BF), 0, 1).astype(F32)
            last_row = self.hop(self.turn(second[1].astype(BF), 2), 2).astype(F32)
            return jnp.concatenate([first[0] + last_col, second[0] + last_row], axis=0)
        sums = {}
        for col_xor in reversed(range(self.cols)):
            for row_xor in reversed(range(0, self.rows, 2)):
                arrived = self.hop(self.turn(blocks[col_xor, row_xor + 1], 1), 1)
                sums[col_xor, row_xor] = blocks[col_xor, row_xor].astype(F32) + arrived.astype(F32)
        total = sums[0, 0]
        for col_xor in reversed(range(self.cols)):
            for row_xor in reversed(range(0, self.rows, 2)):
                if col_xor or row_xor:
                    sent = self.turn(sums[col_xor, row_xor].astype(BF), row_xor)
                    total = total + self.hop(sent, row_xor, col_xor).astype(F32)
        return total

    def total(self, array):
        blocks = array.reshape(array.shape[:-1] + (self.cols, self.rows, -1))
        row_xor = 1
        while row_xor < self.rows:
            order = [index ^ row_xor for index in range(self.rows)]
            arrived = self.hop(blocks, row_xor)
            blocks = blocks + jnp.stack([arrived[..., k, :] for k in order], axis=-2)
            row_xor *= 2
        col_xor = 1
        while col_xor < self.cols:
            order = [index ^ col_xor for index in range(self.cols)]
            arrived = self.hop(blocks, 0, col_xor)
            blocks = blocks + jnp.stack([arrived[..., k, :, :] for k in order], axis=-3)
            col_xor *= 2
        return blocks.reshape(array.shape)


ENDS = [(0, 1), (1, 0), (2, 3), (3, 2)]
MIDDLE = [(1, 2), (2, 1)]


def plus(one, other):
    return (one.astype(F32) + other.astype(F32)).astype(BF)


def group_sums(arrays, lag=3):
    if lax.axis_size("dp") != 4:
        return [lax.psum(array, "dp") for array in arrays]
    place = lax.axis_index("dp")
    inner = (place == 1) | (place == 2)
    count = len(arrays)
    arrived, full, result = {}, {}, {}
    for step in range(count + lag):
        back = step - lag
        array = arrays[step] if step < count else None
        if back >= 0 and array is not None and full[back].shape == array.shape:
            sent = jnp.where(inner, full[back], array)
            arrived[step] = lax.ppermute(sent, "dp", ENDS)
            result[back] = jnp.where(inner, sent, arrived[step])
        else:
            if back >= 0 and array is not None:
                full[back], array = lax.optimization_barrier((full[back], array))
            if array is not None:
                arrived[step] = lax.ppermute(array, "dp", [(0, 1), (3, 2)])
            if back >= 0:
                again = lax.ppermute(full[back], "dp", [(1, 0), (2, 3)])
                result[back] = jnp.where(inner, full[back], again)
        if array is not None:
            pair = plus(array, arrived[step])
            full[step] = plus(pair, lax.ppermute(pair, "dp", MIDDLE))
    return [result[k] for k in range(count)]


def group_total(vector):
    if lax.axis_size("dp") != 4:
        return lax.psum(vector, "dp")
    place = lax.axis_index("dp")
    inner = (place == 1) | (place == 2)
    vector = vector + lax.ppermute(vector, "dp", [(0, 1), (3, 2)])
    vector = vector + lax.ppermute(vector, "dp", MIDDLE)
    return jnp.where(inner, vector, lax.ppermute(vector, "dp", [(1, 0), (2, 3)]))


def shards(
    layer_input,
    cotangent,
    lengths,
    deal_slot,
    query_weight,
    key_weight,
    value_weight,
    out_weight,
    query_gain,
    key_gain,
    attn_gain,
    gate_weight,
    up_weight,
    down_weight,
    mlp_gain,
):
    groups = lax.axis_size("dp")
    my_group = lax.axis_index("dp")
    seq_grp, tok_seq, width = layer_input.shape
    seq_count = lengths.shape[0]
    plane = Plane(width)
    rows, cols, row, col, part = plane.rows, plane.cols, plane.row, plane.col, plane.part
    seq_own = seq_grp // cols
    tok_own = seq_own * tok_seq
    seq_len = tok_seq * rows
    tok_all = seq_grp * seq_len
    heads_cols = query_weight.shape[1]
    head_part = heads_cols // rows
    heads_here = head_part // HD
    ff_part = gate_weight.shape[1] // rows

    first_own = col * seq_own
    all_input = plane.relative(layer_input)
    own_cot = plane.relative(
        lax.dynamic_slice_in_dim(cotangent, first_own, seq_own, axis=0).reshape(tok_own, width)
    )
    own_places = row * tok_seq + jnp.arange(tok_seq, dtype=jnp.int32)
    group_len = lax.dynamic_slice_in_dim(lengths, my_group * seq_grp, seq_grp)
    valid_all = (own_places[None, :] < group_len[:, None]).astype(BF)
    all_input = (all_input * valid_all[:, :, None]).reshape(cols, tok_own, width)
    all_input = jnp.stack(
        [
            lax.dynamic_index_in_dim(all_input, col ^ index, axis=0, keepdims=False)
            for index in range(cols)
        ]
    )
    inputs_low = all_input[0]
    own_len = lax.dynamic_slice_in_dim(lengths, my_group * seq_grp + first_own, seq_own)
    valid_rows = (own_places[None, :] < own_len[:, None]).astype(F32).reshape(tok_own, 1)
    inputs = inputs_low.astype(F32)
    d_full = own_cot.astype(F32) * valid_rows
    inputs_all = plane.gather_columns(all_input)

    def pieces_of(weight, axis):
        size = weight.shape[axis] // rows
        return [
            lax.dynamic_slice_in_dim(weight, (row ^ k) * size, size, axis=axis)
            for k in range(rows)
        ]

    def shared(weight, axis):
        pieces = pieces_of(weight, axis)
        size = pieces[0].shape[0] // groups
        parts = [
            plane.hop(lax.dynamic_slice_in_dim(piece, my_group * size, size, axis=0), k)
            for k, piece in enumerate(pieces)
            if k >= 2
        ]
        far = lax.all_gather(jnp.concatenate(parts, axis=1), "dp", axis=0, tiled=True)
        far = jnp.split(far, rows - 2, axis=1)
        return pieces[:1] + [plane.hop(pieces[1], 1)] + far

    trios = zip(
        pieces_of(query_weight, 1), pieces_of(key_weight, 1), pieces_of(value_weight, 1), strict=True
    )
    trios = [plane.hop(jnp.stack(trio), k) for k, trio in enumerate(trios)]
    w_query, w_key, w_value = (
        jnp.concatenate([trio[k] for trio in trios], axis=0) for k in range(3)
    )
    w_gate = jnp.concatenate(shared(gate_weight, 1), axis=0)
    w_out = jnp.concatenate(
        [plane.hop(piece, k) for k, piece in enumerate(pieces_of(out_weight, 0))], axis=1
    )
    w_up = jnp.concatenate(shared(up_weight, 1), axis=0)
    w_down = jnp.concatenate(shared(down_weight, 0), axis=1)
    gains = jnp.stack([attn_gain, mlp_gain])
    gains = jnp.concatenate([plane.hop(gains, k) for k in range(rows)], axis=1).astype(F32)
    attn_gain_f, mlp_gain_f = gains[0:1], gains[1:2]
    q_gain_f = lax.dynamic_slice_in_dim(query_gain, row * head_part, head_part).astype(F32)
    k_gain_f = lax.dynamic_slice_in_dim(key_gain, row * head_part, head_part).astype(F32)

    def by_sequence(array):
        shape = (cols, rows, seq_own, tok_seq) + array.shape[1:]
        return jnp.swapaxes(array.reshape(shape), 1, 2).reshape(
            (seq_grp, seq_len) + array.shape[1:]
        )

    def by_block(array):
        shape = (cols, seq_own, rows, tok_seq) + array.shape[2:]
        return jnp.swapaxes(array.reshape(shape), 1, 2).reshape((tok_all,) + array.shape[2:])

    query_raw = dot(inputs_all, w_query)
    key_raw = dot(inputs_all, w_key)
    value_low = dot(inputs_all, w_value).astype(BF)
    squares = jnp.stack(
        [jnp.sum(query_raw * query_raw, axis=1), jnp.sum(key_raw * key_raw, axis=1)]
    )
    scales = lax.rsqrt(plane.total(squares) / width + EPSILON)
    q_scale = scales[0][:, None]
    k_scale = scales[1][:, None]
    q_unit = query_raw * q_scale
    k_unit = key_raw * k_scale
    block_rows = row ^ jnp.arange(rows, dtype=jnp.int32)
    places = (
        block_rows[:, None] * tok_seq + jnp.arange(tok_seq, dtype=jnp.int32)[None, :]
    ).reshape(seq_len)
    block_cols = col ^ jnp.arange(cols, dtype=jnp.int32)
    seq_ids = (
        my_group * seq_grp
        + block_cols[:, None] * seq_own
        + jnp.arange(seq_own, dtype=jnp.int32)[None, :]
    ).reshape(seq_grp)
    live_len = jnp.sum(
        jnp.where(
            seq_ids[:, None] == jnp.arange(seq_count, dtype=jnp.int32)[None, :], lengths[None, :], 0
        ),
        axis=1,
    )
    frequency = ROPE_THETA ** (-(jnp.arange(HD // 2).astype(F32) * 2.0 / HD))
    angles = places.astype(F32)[:, None] * frequency[None, :]
    cos_table = jnp.cos(angles)[None, :, None, :]
    sin_table = jnp.sin(angles)[None, :, None, :]
    head_shape = (seq_grp, seq_len, heads_here, HD)

    def heads_of(array):
        return by_sequence(array).reshape(head_shape)

    def joined(array):
        return by_block(array.reshape(seq_grp, seq_len, head_part))

    q_rot = rotate_pairs(heads_of(q_unit * q_gain_f), cos_table, sin_table).astype(BF)
    k_rot = rotate_pairs(heads_of(k_unit * k_gain_f), cos_table, sin_table).astype(BF)
    values = heads_of(value_low)
    allowed = (places[None, None, :] <= places[None, :, None]) & (
        places[None, None, :] < live_len[:, None, None]
    )
    score_scale = HD ** (-0.5)
    scores = (
        jnp.einsum("sqhd,skhd->shqk", q_rot, k_rot, preferred_element_type=F32) * score_scale
    )
    scores = jnp.where(allowed[:, None], scores, -MASK_VALUE)
    exponent = jnp.exp(scores - jnp.max(scores, axis=-1, keepdims=True))
    prob = exponent / jnp.sum(exponent, axis=-1, keepdims=True)
    prob_low = prob.astype(BF)
    attn_mix = joined(
        jnp.einsum("shqk,skhd->sqhd", prob_low, values, preferred_element_type=F32).astype(BF)
    )
    attn_raw = plane.scatter(dot(attn_mix, w_out).astype(BF))
    a_scale = rms_scale(attn_raw)
    a_unit = attn_raw * a_scale
    branch_a = a_unit * attn_gain_f
    hidden = inputs + branch_a
    hidden_all = plane.gather(hidden.astype(BF))
    gate_pre = dot(hidden_all, w_gate)
    up_pre = dot(hidden_all, w_up)
    gate_sig = jax.nn.sigmoid(gate_pre)
    gate_act = gate_pre * gate_sig
    inner_low = (gate_act * up_pre).astype(BF)
    mlp_raw = plane.scatter(dot(inner_low, w_down).astype(BF))
    m_scale = rms_scale(mlp_raw)
    m_unit = mlp_raw * m_scale
    branch_m = m_unit * mlp_gain_f
    result = (hidden + branch_m) * valid_rows

    d_m_unit = d_full * mlp_gain_f
    d_mlp = m_scale * (d_m_unit - m_unit * jnp.mean(d_m_unit * m_unit, axis=-1, keepdims=True))
    d_mlp_all = plane.gather(d_mlp.astype(BF))
    grads_down = [against(inner_low, plane.slot(d_mlp_all, k)).astype(BF) for k in range(rows)]
    d_inner = through(d_mlp_all, w_down)
    d_gate_low = (d_inner * up_pre * (gate_sig * (1.0 + gate_pre * (1.0 - gate_sig)))).astype(BF)
    d_up_low = (d_inner * gate_act).astype(BF)
    grads_gate = [against(plane.slot(hidden_all, k), d_gate_low).astype(BF) for k in range(rows)]
    grads_up = [against(plane.slot(hidden_all, k), d_up_low).astype(BF) for k in range(rows)]
    d_hidden = d_full + plane.scatter(
        (through(d_gate_low, w_gate) + through(d_up_low, w_up)).astype(BF)
    )
    d_a_unit = d_hidden * attn_gain_f
    d_attn = a_scale * (d_a_unit - a_unit * jnp.mean(d_a_unit * a_unit, axis=-1, keepdims=True))
    d_attn_all = plane.gather(d_attn.astype(BF))
    grads_out = against(attn_mix, d_attn_all).astype(BF)
    d_mix = heads_of(through(d_attn_all, w_out).astype(BF))
    d_prob = jnp.einsum("sqhd,skhd->shqk", d_mix, values, preferred_element_type=F32)
    row_delta = jnp.sum(prob * d_prob, axis=-1, keepdims=True)
    d_scores = (prob * (d_prob - row_delta)).astype(BF)
    d_qrot = (
        jnp.einsum("shqk,skhd->sqhd", d_scores, k_rot, preferred_element_type=F32) * score_scale
    )
    d_krot = (
        jnp.einsum("shqk,sqhd->skhd", d_scores, q_rot, preferred_element_type=F32) * score_scale
    )
    d_value = jnp.einsum("shqk,sqhd->skhd", prob_low, d_mix, preferred_element_type=F32)
    d_qn = joined(rotate_pairs(d_qrot, cos_table, -sin_table))
    d_kn = joined(rotate_pairs(d_krot, cos_table, -sin_table))
    d_q_hat = d_qn * q_gain_f
    d_k_hat = d_kn * k_gain_f
    inners = plane.total(
        jnp.stack([jnp.sum(d_q_hat * q_unit, axis=1), jnp.sum(d_k_hat * k_unit, axis=1)])
    )
    d_query = q_scale * (d_q_hat - q_unit * (inners[0] / width)[:, None])
    d_key = k_scale * (d_k_hat - k_unit * (inners[1] / width)[:, None])
    d_query = d_query.astype(BF)
    d_key = d_key.astype(BF)
    d_value = joined(d_value.astype(BF))
    d_qkv = jnp.concatenate([d_query, d_key, d_value], axis=1)
    grads_qkv = [against(plane.slot(inputs_all, k), d_qkv).astype(BF) for k in range(rows)]
    d_inputs = d_hidden + plane.scatter(
        (through(d_query, w_query) + through(d_key, w_key) + through(d_value, w_value)).astype(BF)
    )

    def home(array):
        own = plane.relative((array).astype(BF)).reshape(seq_own, tok_seq, width)
        pieces = [own] + [plane.hop(own, 0, k) for k in range(1, cols)]
        out = jnp.zeros((seq_grp, tok_seq, width), BF)
        for k in range(cols):
            out = lax.dynamic_update_slice_in_dim(out, pieces[k], (col ^ k) * seq_own, axis=0)
        return out

    output = home(result)
    grad_input = home(d_inputs * valid_rows)

    def finish(blocks, axis):
        size = blocks[0].shape[axis]
        shape = list(blocks[0].shape)
        shape[axis] = size * rows
        out = jnp.zeros(shape, F32)
        for k in reversed(range(rows)):
            start = [0, 0]
            start[axis] = (row ^ k) * size
            out = lax.dynamic_update_slice(out, blocks[k].astype(F32), start)
        return out

    order = [k for k in range(2, rows)] + [1, 0]
    chunks = [grads[k] for grads in (grads_down, grads_gate, grads_up) for k in order]
    chunks += [grads_out] + [grads_qkv[k] for k in order]
    summed = group_sums(chunks)

    def arrived_at(blocks):
        placed = [plane.hop(block, k) for k, block in zip(order, blocks, strict=True)]
        return [placed[order.index(k)] for k in range(rows)]

    grad_down = finish(arrived_at(summed[:rows]), 0)
    grad_gate = finish(arrived_at(summed[rows : 2 * rows]), 1)
    grad_up = finish(arrived_at(summed[2 * rows : 3 * rows]), 1)
    grad_out = finish(arrived_at([plane.slot(summed[3 * rows], k) for k in order]), 0)
    qkv_blocks = arrived_at(summed[3 * rows + 1 :])
    grad_query = finish([b[:, :head_part] for b in qkv_blocks], 1)
    grad_key = finish([b[:, head_part : 2 * head_part] for b in qkv_blocks], 1)
    grad_value = finish([b[:, 2 * head_part :] for b in qkv_blocks], 1)

    def sums_of(array):
        return jnp.sum(array.reshape(seq_own, tok_seq * width), axis=1)

    own_sums = jnp.stack(
        [
            sums_of(result * result),
            sums_of(branch_a * branch_a * valid_rows),
            sums_of(branch_m * branch_m * valid_rows),
        ],
        axis=1,
    )
    own_ids = my_group * seq_grp + first_own + jnp.arange(seq_own, dtype=jnp.int32)
    seq_sums = jnp.sum(
        jnp.where(
            own_ids[:, None, None] == jnp.arange(seq_count, dtype=jnp.int32)[None, :, None],
            own_sums[:, None, :],
            0.0,
        ),
        axis=0,
    )
    gain_sums = plane.relative(
        jnp.stack([jnp.sum(d_hidden * a_unit, axis=0), jnp.sum(d_full * m_unit, axis=0)])
    )
    head_sums = jnp.stack([jnp.sum(d_qn * q_unit, axis=0), jnp.sum(d_kn * k_unit, axis=0)])
    mine = (
        (jnp.arange(cols)[:, None] == col) & (jnp.arange(rows)[None, :] == row)
    ).astype(F32)
    head_sums = (head_sums[:, None, None, :] * mine[None, :, :, None]).reshape(2, cols, heads_cols)
    vector = jnp.concatenate([gain_sums.reshape(-1), head_sums.reshape(-1), seq_sums.reshape(-1)])
    vector = jnp.pad(vector, (0, -vector.shape[0] % 1024)).reshape(-1, 1024)
    row_xor = 1
    while row_xor < rows:
        vector = vector + plane.hop(vector, row_xor)
        row_xor *= 2
    col_xor = 1
    while col_xor < cols:
        vector = vector + plane.hop(vector, 0, col_xor)
        col_xor *= 2
    vector = group_total(vector).reshape(-1)
    gain_sums = lax.dynamic_slice_in_dim(
        vector[: 2 * width].reshape(2, width), row * part, part, axis=1
    )
    head_end = 2 * width + 2 * cols * heads_cols
    head_sums = lax.dynamic_slice_in_dim(
        vector[2 * width : head_end].reshape(2, cols, heads_cols), col, 1, axis=1
    )
    seq_sums = vector[head_end : head_end + 3 * seq_count].reshape(seq_count, 3)
    member = (
        (deal_slot // seq_grp)[:, None] == jnp.arange(groups, dtype=jnp.int32)[None, :]
    ).astype(F32)
    counts = jnp.sum(member * lengths.astype(F32)[:, None], axis=0)
    stat_sums = jnp.sum(member[:, :, None] * seq_sums[:, None, :], axis=0)
    rms_stats = jnp.sqrt(stat_sums / (counts[:, None] * width))
    return (
        output,
        grad_input,
        grad_query,
        grad_key,
        grad_value,
        grad_out,
        head_sums[0, 0],
        head_sums[1, 0],
        gain_sums[0],
        grad_gate,
        grad_up,
        grad_down,
        gain_sums[1],
        rms_stats,
    )


def solution(mesh):
    tokens = P("dp", "row", None)
    inward = P("row", "col")
    outward = P("col", "row")
    in_specs = (
        (tokens, tokens, P(), P())
        + (inward, inward, inward, outward)
        + (P("col"), P("col"), P("row"))
        + (inward, inward, outward, P("row"))
    )
    out_specs = (
        (tokens, tokens)
        + (inward, inward, inward, outward)
        + (P("col"), P("col"), P("row"))
        + (inward, inward, outward, P("row"))
        + (P(),)
    )
    return jax.shard_map(shards, mesh=mesh, in_specs=in_specs, out_specs=out_specs, check_vma=False)
```

```python
import jax
import jax.numpy as jnp
from jax import lax
from jax.sharding import PartitionSpec as P

HD = 128
EPSILON = 1e-06
ROPE_THETA = 500000.0
MASK_VALUE = 1e30
BF = jnp.bfloat16
F32 = jnp.float32


def rms_scale(matrix):
    return lax.rsqrt(jnp.mean(matrix * matrix, axis=-1, keepdims=True) + EPSILON)


def rotate_pairs(matrix, cos_table, sin_table):
    half_size = matrix.shape[-1] // 2
    first_half = matrix[..., :half_size]
    second_half = matrix[..., half_size:]
    return jnp.concatenate(
        [
            first_half * cos_table - second_half * sin_table,
            second_half * cos_table + first_half * sin_table,
        ],
        axis=-1,
    )


def dot(left_side, right_side):
    return jnp.dot(left_side, right_side, preferred_element_type=F32)


def against(left_side, right_side):
    return lax.dot_general(
        left_side, right_side, (((0,), (0,)), ((), ())), preferred_element_type=F32
    )


def through(left_side, weight):
    return lax.dot_general(
        left_side, weight, (((1,), (1,)), ((), ())), preferred_element_type=F32
    )


def together(*values):
    return lax.optimization_barrier(values)


def unchanged(value):
    return value


class Plane:
    def __init__(self, width):
        self.rows = lax.axis_size("row")
        self.cols = lax.axis_size("col")
        self.row = lax.axis_index("row")
        self.col = lax.axis_index("col")
        self.part = width // self.rows

    def hop(self, array, row_xor, col_xor=0):
        if row_xor and col_xor:
            pairs = [
                (a * self.cols + b, (a ^ row_xor) * self.cols + (b ^ col_xor))
                for a in range(self.rows)
                for b in range(self.cols)
            ]
            return lax.ppermute(array, ("row", "col"), pairs)
        if row_xor:
            return lax.ppermute(array, "row", [(a, a ^ row_xor) for a in range(self.rows)])
        if col_xor:
            return lax.ppermute(array, "col", [(a, a ^ col_xor) for a in range(self.cols)])
        return array

    def slot(self, array, index):
        return array[..., index * self.part : (index + 1) * self.part]

    def turn(self, array, row_xor):
        if row_xor == 0:
            return array
        return jnp.concatenate(
            [self.slot(array, index ^ row_xor) for index in range(self.rows)], axis=-1
        )

    def relative(self, array):
        return jnp.concatenate(
            [
                lax.dynamic_slice_in_dim(
                    array, (self.row ^ index) * self.part, self.part, axis=array.ndim - 1
                )
                for index in range(self.rows)
            ],
            axis=-1,
        )

    def gather(self, own, step=unchanged):
        blocks = {(0, 0): own}
        if self.rows == 4 and self.cols == 2:
            half = own.shape[0] // 2
            blocks[0, 2] = self.hop(self.turn(own, 2), 2)
            blocks[1, 0] = self.hop(own, 0, 1)
            blocks = step(blocks)
            blocks[1, 2] = jnp.concatenate(
                [
                    self.hop(blocks[0, 2][:half], 0, 1),
                    self.hop(self.turn(blocks[1, 0][half:], 2), 2),
                ],
                axis=0,
            )
        else:
            for col_xor in reversed(range(self.cols)):
                for row_xor in reversed(range(0, self.rows, 2)):
                    blocks[col_xor, row_xor] = self.hop(self.turn(own, row_xor), row_xor, col_xor)
        return step(self.over_cores(blocks))

    def over_cores(self, blocks):
        for col_xor in range(self.cols):
            for row_xor in range(0, self.rows, 2):
                blocks[col_xor, row_xor + 1] = self.hop(
                    self.turn(blocks[col_xor, row_xor], 1), 1
                )
        return jnp.concatenate(
            [blocks[b, a] for b in range(self.cols) for a in range(self.rows)], axis=0
        )

    def gather_columns(self, own):
        blocks = {}
        for row_xor in range(0, self.rows, 2):
            arrived = self.hop(self.turn(own[0], row_xor), row_xor)
            for col_xor in range(self.cols):
                if row_xor:
                    blocks[col_xor, row_xor] = self.hop(arrived, 0, col_xor)
                else:
                    blocks[col_xor, row_xor] = own[col_xor]
        return self.over_cores(blocks)

    def scatter(self, partial, step=unchanged):
        tokens = partial.shape[0] // (self.rows * self.cols)
        blocks = partial.reshape(self.cols, self.rows, tokens, -1)
        if self.rows == 4 and self.cols == 2:
            half = tokens // 2
            away = self.hop(self.turn(jnp.stack([blocks[:, 1], blocks[:, 3]]), 1), 1)
            away, blocks = step((away, blocks))
            near = [blocks[:, 2 * k].astype(F32) + away[k].astype(F32) for k in range(2)]
            by_row = self.hop(self.turn(near[1][:, :half].astype(BF), 2), 2)
            far = jnp.stack([near[0][1, half:], near[1][1, half:]]).astype(BF)
            by_col = self.hop(far, 0, 1)
            by_row, by_col, near = step((by_row, by_col, near))
            first = [near[0][k, :half] + by_row[k].astype(F32) for k in range(2)]
            second = [near[k][0, half:] + by_col[k].astype(F32) for k in range(2)]
            last_col = self.hop(first[1].astype(BF), 0, 1).astype(F32)
            last_row = self.hop(self.turn(second[1].astype(BF), 2), 2).astype(F32)
            return step(jnp.concatenate([first[0] + last_col, second[0] + last_row], axis=0))
        sums = {}
        for col_xor in reversed(range(self.cols)):
            for row_xor in reversed(range(0, self.rows, 2)):
                arrived = self.hop(self.turn(blocks[col_xor, row_xor + 1], 1), 1)
                sums[col_xor, row_xor] = blocks[col_xor, row_xor].astype(F32) + arrived.astype(F32)
        total = sums[0, 0]
        for col_xor in reversed(range(self.cols)):
            for row_xor in reversed(range(0, self.rows, 2)):
                if col_xor or row_xor:
                    sent = self.turn(sums[col_xor, row_xor].astype(BF), row_xor)
                    total = total + self.hop(sent, row_xor, col_xor).astype(F32)
        return total

    def total(self, array):
        blocks = array.reshape(array.shape[:-1] + (self.cols, self.rows, -1))
        row_xor = 1
        while row_xor < self.rows:
            order = [index ^ row_xor for index in range(self.rows)]
            arrived = self.hop(blocks, row_xor)
            blocks = blocks + jnp.stack([arrived[..., k, :] for k in order], axis=-2)
            row_xor *= 2
        col_xor = 1
        while col_xor < self.cols:
            order = [index ^ col_xor for index in range(self.cols)]
            arrived = self.hop(blocks, 0, col_xor)
            blocks = blocks + jnp.stack([arrived[..., k, :, :] for k in order], axis=-3)
            col_xor *= 2
        return blocks.reshape(array.shape)


ENDS = [(0, 1), (1, 0), (2, 3), (3, 2)]
MIDDLE = [(1, 2), (2, 1)]


def plus(one, other):
    return (one.astype(F32) + other.astype(F32)).astype(BF)


class Line:
    depth = 2

    def __init__(self, move):
        self.line = lax.axis_size("dp") == 4
        place = lax.axis_index("dp")
        self.inner = (place == 1) | (place == 2)
        self.move = move
        self.arrays, self.pairs, self.full, self.placed = [], [], [], []
        self.pending = [{}] * self.depth
        self.moving = [[]] * (self.depth + 1)
        self.sent_back = 0

    def step(self, values, array=None):
        if not self.line:
            if array is not None:
                self.arrays.append(array)
            return values
        pending, moving, array, values = lax.optimization_barrier(
            (self.pending.pop(0), self.moving.pop(0), array, values)
        )
        self.advance(pending, moving, array)
        return values

    def advance(self, pending, moving, array):
        self.placed += moving
        current, moved = {}, []
        if "back" in pending:
            total = jnp.where(self.inner, pending["full"], pending["back"])
            moved.append(self.move(len(self.placed) + sum(map(len, self.moving)), total))
        self.moving.append(moved)
        if "across" in pending:
            self.full.append(plus(self.pairs[len(self.full)], pending["across"]))
        if "inward" in pending:
            pair = plus(self.arrays[len(self.pairs)], pending["inward"])
            self.pairs.append(pair)
            current["across"] = lax.ppermute(pair, "dp", MIDDLE)
        back = None
        if len(self.full) > self.sent_back:
            back = self.full[self.sent_back]
            self.sent_back += 1
        if array is not None:
            self.arrays.append(array)
        if back is not None and array is not None and back.shape == array.shape:
            sent = jnp.where(self.inner, back, array)
            current["full"] = sent
            current["inward"] = lax.ppermute(sent, "dp", ENDS)
            current["back"] = current["inward"]
        else:
            if array is not None:
                current["inward"] = lax.ppermute(array, "dp", [(0, 1), (3, 2)])
            if back is not None:
                current["full"] = back
                current["back"] = lax.ppermute(back, "dp", [(1, 0), (2, 3)])
        self.pending.append(current)

    def finish(self):
        if not self.line:
            totals = [lax.psum(array, "dp") for array in self.arrays]
            return [self.move(index, total) for index, total in enumerate(totals)]
        while len(self.placed) < len(self.arrays):
            self.advance(self.pending.pop(0), self.moving.pop(0), None)
        return self.placed


def group_total(vector):
    if lax.axis_size("dp") != 4:
        return lax.psum(vector, "dp")
    place = lax.axis_index("dp")
    inner = (place == 1) | (place == 2)
    vector = vector + lax.ppermute(vector, "dp", [(0, 1), (3, 2)])
    vector = vector + lax.ppermute(vector, "dp", MIDDLE)
    return jnp.where(inner, vector, lax.ppermute(vector, "dp", [(1, 0), (2, 3)]))


def shards(
    layer_input,
    cotangent,
    lengths,
    deal_slot,
    query_weight,
    key_weight,
    value_weight,
    out_weight,
    query_gain,
    key_gain,
    attn_gain,
    gate_weight,
    up_weight,
    down_weight,
    mlp_gain,
):
    groups = lax.axis_size("dp")
    my_group = lax.axis_index("dp")
    seq_grp, tok_seq, width = layer_input.shape
    seq_count = lengths.shape[0]
    plane = Plane(width)
    rows, cols, row, col, part = plane.rows, plane.cols, plane.row, plane.col, plane.part
    seq_own = seq_grp // cols
    tok_own = seq_own * tok_seq
    seq_len = tok_seq * rows
    tok_all = seq_grp * seq_len
    heads_cols = query_weight.shape[1]
    head_part = heads_cols // rows
    heads_here = head_part // HD
    ff_part = gate_weight.shape[1] // rows

    first_own = col * seq_own
    all_input = plane.relative(layer_input)
    own_cot = plane.relative(
        lax.dynamic_slice_in_dim(cotangent, first_own, seq_own, axis=0).reshape(tok_own, width)
    )
    own_places = row * tok_seq + jnp.arange(tok_seq, dtype=jnp.int32)
    group_len = lax.dynamic_slice_in_dim(lengths, my_group * seq_grp, seq_grp)
    valid_all = (own_places[None, :] < group_len[:, None]).astype(BF)
    all_input = (all_input * valid_all[:, :, None]).reshape(cols, tok_own, width)
    all_input = jnp.stack(
        [
            lax.dynamic_index_in_dim(all_input, col ^ index, axis=0, keepdims=False)
            for index in range(cols)
        ]
    )
    inputs_low = all_input[0]
    own_len = lax.dynamic_slice_in_dim(lengths, my_group * seq_grp + first_own, seq_own)
    valid_rows = (own_places[None, :] < own_len[:, None]).astype(F32).reshape(tok_own, 1)
    inputs = inputs_low.astype(F32)
    d_full = own_cot.astype(F32) * valid_rows
    inputs_all = plane.gather_columns(all_input)

    def pieces_of(weight, axis):
        size = weight.shape[axis] // rows
        return [
            lax.dynamic_slice_in_dim(weight, (row ^ k) * size, size, axis=axis)
            for k in range(rows)
        ]

    def shared(weight, axis):
        pieces = pieces_of(weight, axis)
        size = pieces[0].shape[0] // groups
        parts = [
            plane.hop(lax.dynamic_slice_in_dim(piece, my_group * size, size, axis=0), k)
            for k, piece in enumerate(pieces)
            if k >= 2
        ]
        return pieces[:1] + [plane.hop(pieces[1], 1)], jnp.concatenate(parts, axis=1)

    def whole(pieces, far, axis):
        return jnp.concatenate(pieces + jnp.split(far, rows - 2, axis=1), axis=axis)

    def over_groups(part):
        return lax.all_gather(part, "dp", axis=0, tiled=True)

    gate_pieces, gate_far = shared(gate_weight, 1)
    trios = [
        jnp.stack(trio)
        for trio in zip(
            pieces_of(query_weight, 1),
            pieces_of(key_weight, 1),
            pieces_of(value_weight, 1),
            strict=True,
        )
    ]
    gate_far, trios[2:] = together(gate_far, trios[2:])
    gate_far = over_groups(gate_far)
    trios = [plane.hop(trio, k) for k, trio in enumerate(trios)]
    gate_far, trios, inputs_all = together(gate_far, trios, inputs_all)
    up_pieces, up_far = shared(up_weight, 1)
    down_pieces, down_far = shared(down_weight, 0)
    w_query, w_key, w_value = (
        jnp.concatenate([trio[k] for trio in trios], axis=0) for k in range(3)
    )
    w_out = jnp.concatenate(
        [plane.hop(piece, k) for k, piece in enumerate(pieces_of(out_weight, 0))], axis=1
    )
    gains = jnp.stack([attn_gain, mlp_gain])
    gains = jnp.concatenate([plane.hop(gains, k) for k in range(rows)], axis=1).astype(F32)
    attn_gain_f, mlp_gain_f = gains[0:1], gains[1:2]
    q_gain_f = lax.dynamic_slice_in_dim(query_gain, row * head_part, head_part).astype(F32)
    k_gain_f = lax.dynamic_slice_in_dim(key_gain, row * head_part, head_part).astype(F32)

    def by_sequence(array):
        shape = (cols, rows, seq_own, tok_seq) + array.shape[1:]
        return jnp.swapaxes(array.reshape(shape), 1, 2).reshape(
            (seq_grp, seq_len) + array.shape[1:]
        )

    def by_block(array):
        shape = (cols, seq_own, rows, tok_seq) + array.shape[2:]
        return jnp.swapaxes(array.reshape(shape), 1, 2).reshape((tok_all,) + array.shape[2:])

    query_raw = dot(inputs_all, w_query)
    key_raw = dot(inputs_all, w_key)
    value_low = dot(inputs_all, w_value).astype(BF)
    squares = jnp.stack(
        [jnp.sum(query_raw * query_raw, axis=1), jnp.sum(key_raw * key_raw, axis=1)]
    )
    scales = lax.rsqrt(plane.total(squares) / width + EPSILON)
    q_scale = scales[0][:, None]
    k_scale = scales[1][:, None]
    q_unit = query_raw * q_scale
    k_unit = key_raw * k_scale
    block_rows = row ^ jnp.arange(rows, dtype=jnp.int32)
    places = (
        block_rows[:, None] * tok_seq + jnp.arange(tok_seq, dtype=jnp.int32)[None, :]
    ).reshape(seq_len)
    block_cols = col ^ jnp.arange(cols, dtype=jnp.int32)
    seq_ids = (
        my_group * seq_grp
        + block_cols[:, None] * seq_own
        + jnp.arange(seq_own, dtype=jnp.int32)[None, :]
    ).reshape(seq_grp)
    live_len = jnp.sum(
        jnp.where(
            seq_ids[:, None] == jnp.arange(seq_count, dtype=jnp.int32)[None, :], lengths[None, :], 0
        ),
        axis=1,
    )
    frequency = ROPE_THETA ** (-(jnp.arange(HD // 2).astype(F32) * 2.0 / HD))
    angles = places.astype(F32)[:, None] * frequency[None, :]
    cos_table = jnp.cos(angles)[None, :, None, :]
    sin_table = jnp.sin(angles)[None, :, None, :]
    head_shape = (seq_grp, seq_len, heads_here, HD)

    def heads_of(array):
        return by_sequence(array).reshape(head_shape)

    def joined(array):
        return by_block(array.reshape(seq_grp, seq_len, head_part))

    q_rot = rotate_pairs(heads_of(q_unit * q_gain_f), cos_table, sin_table).astype(BF)
    k_rot = rotate_pairs(heads_of(k_unit * k_gain_f), cos_table, sin_table).astype(BF)
    values = heads_of(value_low)
    up_far, q_rot = together(up_far, q_rot)
    up_far = over_groups(up_far)
    allowed = (places[None, None, :] <= places[None, :, None]) & (
        places[None, None, :] < live_len[:, None, None]
    )
    score_scale = HD ** (-0.5)
    scores = (
        jnp.einsum("sqhd,skhd->shqk", q_rot, k_rot, preferred_element_type=F32) * score_scale
    )
    scores = jnp.where(allowed[:, None], scores, -MASK_VALUE)
    exponent = jnp.exp(scores - jnp.max(scores, axis=-1, keepdims=True))
    prob = exponent / jnp.sum(exponent, axis=-1, keepdims=True)
    prob_low = prob.astype(BF)
    attn_mix = joined(
        jnp.einsum("shqk,skhd->sqhd", prob_low, values, preferred_element_type=F32).astype(BF)
    )
    up_far, down_far, attn_mix = together(up_far, down_far, attn_mix)
    down_far = over_groups(down_far)
    attn_raw = plane.scatter(dot(attn_mix, w_out).astype(BF))
    down_far, attn_raw = together(down_far, attn_raw)
    w_gate = whole(gate_pieces, gate_far, 0)
    w_up = whole(up_pieces, up_far, 0)
    w_down = whole(down_pieces, down_far, 1)
    a_scale = rms_scale(attn_raw)
    a_unit = attn_raw * a_scale
    branch_a = a_unit * attn_gain_f
    hidden = inputs + branch_a
    hidden_all = plane.gather(hidden.astype(BF))
    gate_pre = dot(hidden_all, w_gate)
    up_pre = dot(hidden_all, w_up)
    gate_sig = jax.nn.sigmoid(gate_pre)
    gate_act = gate_pre * gate_sig
    inner_low = (gate_act * up_pre).astype(BF)
    mlp_raw = plane.scatter(dot(inner_low, w_down).astype(BF))
    m_scale = rms_scale(mlp_raw)
    m_unit = mlp_raw * m_scale
    branch_m = m_unit * mlp_gain_f
    result = (hidden + branch_m) * valid_rows

    d_m_unit = d_full * mlp_gain_f
    d_mlp = m_scale * (d_m_unit - m_unit * jnp.mean(d_m_unit * m_unit, axis=-1, keepdims=True))
    d_mlp_all = plane.gather(d_mlp.astype(BF))
    order = [k for k in range(2, rows)] + [1, 0]
    waiting = []

    def move(index, total):
        if index < 3 * rows:
            return plane.hop(total, order[index % rows])
        if index == 3 * rows:
            return [plane.hop(plane.slot(total, k), k) for k in order]
        return plane.hop(total, order[(index - 3 * rows - 1) % rows])

    line = Line(move)

    def step(values):
        return line.step(values, waiting.pop(0) if waiting else None)

    waiting += [against(inner_low, plane.slot(d_mlp_all, k)).astype(BF) for k in order]
    d_mlp_all = step(d_mlp_all)
    d_inner = through(d_mlp_all, w_down)
    d_gate_low = (d_inner * up_pre * (gate_sig * (1.0 + gate_pre * (1.0 - gate_sig)))).astype(BF)
    d_up_low = (d_inner * gate_act).astype(BF)
    d_gate_low, d_up_low = step((d_gate_low, d_up_low))
    waiting += [against(plane.slot(hidden_all, k), d_gate_low).astype(BF) for k in order]
    waiting += [against(plane.slot(hidden_all, k), d_up_low).astype(BF) for k in order]
    partial = step((through(d_gate_low, w_gate) + through(d_up_low, w_up)).astype(BF))
    d_hidden = d_full + plane.scatter(partial, step)
    d_a_unit = d_hidden * attn_gain_f
    d_attn = a_scale * (d_a_unit - a_unit * jnp.mean(d_a_unit * a_unit, axis=-1, keepdims=True))
    d_attn_all = plane.gather(d_attn.astype(BF), step)
    waiting += [against(attn_mix, d_attn_all).astype(BF)]
    d_mix = heads_of(through(d_attn_all, w_out).astype(BF))
    d_prob = jnp.einsum("sqhd,skhd->shqk", d_mix, values, preferred_element_type=F32)
    row_delta = jnp.sum(prob * d_prob, axis=-1, keepdims=True)
    d_scores = step((prob * (d_prob - row_delta)).astype(BF))
    d_qrot = (
        jnp.einsum("shqk,skhd->sqhd", d_scores, k_rot, preferred_element_type=F32) * score_scale
    )
    d_krot = (
        jnp.einsum("shqk,sqhd->skhd", d_scores, q_rot, preferred_element_type=F32) * score_scale
    )
    d_value = jnp.einsum("shqk,sqhd->skhd", prob_low, d_mix, preferred_element_type=F32)
    d_qn = joined(rotate_pairs(d_qrot, cos_table, -sin_table))
    d_kn = joined(rotate_pairs(d_krot, cos_table, -sin_table))
    d_value = joined(d_value.astype(BF))
    d_q_hat = d_qn * q_gain_f
    d_k_hat = d_kn * k_gain_f
    d_q_hat, d_k_hat, d_value = step((d_q_hat, d_k_hat, d_value))
    inners = plane.total(
        jnp.stack([jnp.sum(d_q_hat * q_unit, axis=1), jnp.sum(d_k_hat * k_unit, axis=1)])
    )
    inners = step(inners)
    d_query = q_scale * (d_q_hat - q_unit * (inners[0] / width)[:, None])
    d_key = k_scale * (d_k_hat - k_unit * (inners[1] / width)[:, None])
    d_query = d_query.astype(BF)
    d_key = d_key.astype(BF)
    d_qkv = jnp.concatenate([d_query, d_key, d_value], axis=1)
    waiting += [against(plane.slot(inputs_all, k), d_qkv).astype(BF) for k in order]
    partial = step(
        (through(d_query, w_query) + through(d_key, w_key) + through(d_value, w_value)).astype(BF)
    )
    d_inputs = d_hidden + plane.scatter(partial, step)
    while waiting:
        d_inputs = step(d_inputs)

    def finish(blocks, axis):
        size = blocks[0].shape[axis]
        shape = list(blocks[0].shape)
        shape[axis] = size * rows
        out = jnp.zeros(shape, F32)
        for k in reversed(range(rows)):
            start = [0, 0]
            start[axis] = (row ^ k) * size
            out = lax.dynamic_update_slice(out, blocks[k].astype(F32), start)
        return out

    line.placed, d_inputs = lax.optimization_barrier((line.placed, d_inputs))
    placed = line.finish()

    def arrived_at(blocks):
        return [blocks[order.index(k)] for k in range(rows)]

    grad_down = finish(arrived_at(placed[:rows]), 0)
    grad_gate = finish(arrived_at(placed[rows : 2 * rows]), 1)
    grad_up = finish(arrived_at(placed[2 * rows : 3 * rows]), 1)
    grad_out = finish(arrived_at(placed[3 * rows]), 0)
    qkv_blocks = arrived_at(placed[3 * rows + 1 :])
    grad_query = finish([b[:, :head_part] for b in qkv_blocks], 1)
    grad_key = finish([b[:, head_part : 2 * head_part] for b in qkv_blocks], 1)
    grad_value = finish([b[:, 2 * head_part :] for b in qkv_blocks], 1)

    def home(array):
        own = plane.relative((array).astype(BF)).reshape(seq_own, tok_seq, width)
        pieces = [own] + [plane.hop(own, 0, k) for k in range(1, cols)]
        out = jnp.zeros((seq_grp, tok_seq, width), BF)
        for k in range(cols):
            out = lax.dynamic_update_slice_in_dim(out, pieces[k], (col ^ k) * seq_own, axis=0)
        return out

    output = home(result)
    grad_input = home(d_inputs * valid_rows)

    def sums_of(array):
        return jnp.sum(array.reshape(seq_own, tok_seq * width), axis=1)

    own_sums = jnp.stack(
        [
            sums_of(result * result),
            sums_of(branch_a * branch_a * valid_rows),
            sums_of(branch_m * branch_m * valid_rows),
        ],
        axis=1,
    )
    own_ids = my_group * seq_grp + first_own + jnp.arange(seq_own, dtype=jnp.int32)
    seq_sums = jnp.sum(
        jnp.where(
            own_ids[:, None, None] == jnp.arange(seq_count, dtype=jnp.int32)[None, :, None],
            own_sums[:, None, :],
            0.0,
        ),
        axis=0,
    )
    gain_sums = plane.relative(
        jnp.stack([jnp.sum(d_hidden * a_unit, axis=0), jnp.sum(d_full * m_unit, axis=0)])
    )
    head_sums = jnp.stack([jnp.sum(d_qn * q_unit, axis=0), jnp.sum(d_kn * k_unit, axis=0)])
    mine = (
        (jnp.arange(cols)[:, None] == col) & (jnp.arange(rows)[None, :] == row)
    ).astype(F32)
    head_sums = (head_sums[:, None, None, :] * mine[None, :, :, None]).reshape(2, cols, heads_cols)
    vector = jnp.concatenate([gain_sums.reshape(-1), head_sums.reshape(-1), seq_sums.reshape(-1)])
    vector = jnp.pad(vector, (0, -vector.shape[0] % 1024)).reshape(-1, 1024)
    row_xor = 1
    while row_xor < rows:
        vector = vector + plane.hop(vector, row_xor)
        row_xor *= 2
    col_xor = 1
    while col_xor < cols:
        vector = vector + plane.hop(vector, 0, col_xor)
        col_xor *= 2
    vector = group_total(vector).reshape(-1)
    gain_sums = lax.dynamic_slice_in_dim(
        vector[: 2 * width].reshape(2, width), row * part, part, axis=1
    )
    head_end = 2 * width + 2 * cols * heads_cols
    head_sums = lax.dynamic_slice_in_dim(
        vector[2 * width : head_end].reshape(2, cols, heads_cols), col, 1, axis=1
    )
    seq_sums = vector[head_end : head_end + 3 * seq_count].reshape(seq_count, 3)
    member = (
        (deal_slot // seq_grp)[:, None] == jnp.arange(groups, dtype=jnp.int32)[None, :]
    ).astype(F32)
    counts = jnp.sum(member * lengths.astype(F32)[:, None], axis=0)
    stat_sums = jnp.sum(member[:, :, None] * seq_sums[:, None, :], axis=0)
    rms_stats = jnp.sqrt(stat_sums / (counts[:, None] * width))
    return (
        output,
        grad_input,
        grad_query,
        grad_key,
        grad_value,
        grad_out,
        head_sums[0, 0],
        head_sums[1, 0],
        gain_sums[0],
        grad_gate,
        grad_up,
        grad_down,
        gain_sums[1],
        rms_stats,
    )


def solution(mesh):
    tokens = P("dp", "row", None)
    inward = P("row", "col")
    outward = P("col", "row")
    in_specs = (
        (tokens, tokens, P(), P())
        + (inward, inward, inward, outward)
        + (P("col"), P("col"), P("row"))
        + (inward, inward, outward, P("row"))
    )
    out_specs = (
        (tokens, tokens)
        + (inward, inward, inward, outward)
        + (P("col"), P("col"), P("row"))
        + (inward, inward, outward, P("row"))
        + (P(),)
    )
    return jax.shard_map(shards, mesh=mesh, in_specs=in_specs, out_specs=out_specs, check_vma=False)
```

```python
import jax
import jax.numpy as jnp
from jax import lax
from jax.sharding import PartitionSpec as P

HD = 128
EPSILON = 1e-06
ROPE_THETA = 500000.0
MASK_VALUE = 1e30
BF = jnp.bfloat16
F32 = jnp.float32


def rms_scale(matrix):
    return lax.rsqrt(jnp.mean(matrix * matrix, axis=-1, keepdims=True) + EPSILON)


def rotate_pairs(matrix, cos_table, sin_table):
    half_size = matrix.shape[-1] // 2
    first_half = matrix[..., :half_size]
    second_half = matrix[..., half_size:]
    return jnp.concatenate(
        [
            first_half * cos_table - second_half * sin_table,
            second_half * cos_table + first_half * sin_table,
        ],
        axis=-1,
    )


def dot(left_side, right_side):
    return jnp.dot(left_side, right_side, preferred_element_type=F32)


def against(left_side, right_side):
    return lax.dot_general(
        left_side, right_side, (((0,), (0,)), ((), ())), preferred_element_type=F32
    )


def through(left_side, weight):
    return lax.dot_general(
        left_side, weight, (((1,), (1,)), ((), ())), preferred_element_type=F32
    )


def together(*values):
    return lax.optimization_barrier(values)


def unchanged(value):
    return value


class Plane:
    def __init__(self, width):
        self.rows = lax.axis_size("row")
        self.cols = lax.axis_size("col")
        self.row = lax.axis_index("row")
        self.col = lax.axis_index("col")
        self.part = width // self.rows

    def hop(self, array, row_xor, col_xor=0):
        if row_xor and col_xor:
            pairs = [
                (a * self.cols + b, (a ^ row_xor) * self.cols + (b ^ col_xor))
                for a in range(self.rows)
                for b in range(self.cols)
            ]
            return lax.ppermute(array, ("row", "col"), pairs)
        if row_xor:
            return lax.ppermute(array, "row", [(a, a ^ row_xor) for a in range(self.rows)])
        if col_xor:
            return lax.ppermute(array, "col", [(a, a ^ col_xor) for a in range(self.cols)])
        return array

    def slot(self, array, index):
        return array[..., index * self.part : (index + 1) * self.part]

    def turn(self, array, row_xor):
        if row_xor == 0:
            return array
        return jnp.concatenate(
            [self.slot(array, index ^ row_xor) for index in range(self.rows)], axis=-1
        )

    def relative(self, array):
        return jnp.concatenate(
            [
                lax.dynamic_slice_in_dim(
                    array, (self.row ^ index) * self.part, self.part, axis=array.ndim - 1
                )
                for index in range(self.rows)
            ],
            axis=-1,
        )

    def gather(self, own, step=unchanged):
        blocks = {(0, 0): own}
        if self.rows == 4 and self.cols == 2:
            half = own.shape[0] // 2
            blocks[0, 2] = self.hop(self.turn(own, 2), 2)
            blocks[1, 0] = self.hop(own, 0, 1)
            blocks = step(blocks)
            blocks[1, 2] = jnp.concatenate(
                [
                    self.hop(blocks[0, 2][:half], 0, 1),
                    self.hop(self.turn(blocks[1, 0][half:], 2), 2),
                ],
                axis=0,
            )
        else:
            for col_xor in reversed(range(self.cols)):
                for row_xor in reversed(range(0, self.rows, 2)):
                    blocks[col_xor, row_xor] = self.hop(self.turn(own, row_xor), row_xor, col_xor)
        return step(self.over_cores(blocks))

    def over_cores(self, blocks):
        for col_xor in range(self.cols):
            for row_xor in range(0, self.rows, 2):
                blocks[col_xor, row_xor + 1] = self.hop(
                    self.turn(blocks[col_xor, row_xor], 1), 1
                )
        return jnp.concatenate(
            [blocks[b, a] for b in range(self.cols) for a in range(self.rows)], axis=0
        )

    def gather_columns(self, own):
        blocks = {}
        for row_xor in range(0, self.rows, 2):
            arrived = self.hop(self.turn(own[0], row_xor), row_xor)
            for col_xor in range(self.cols):
                if row_xor:
                    blocks[col_xor, row_xor] = self.hop(arrived, 0, col_xor)
                else:
                    blocks[col_xor, row_xor] = own[col_xor]
        return self.over_cores(blocks)

    def scatter(self, partial, step=unchanged):
        tokens = partial.shape[0] // (self.rows * self.cols)
        blocks = partial.reshape(self.cols, self.rows, tokens, -1)
        if self.rows == 4 and self.cols == 2:
            half = tokens // 2
            away = self.hop(self.turn(jnp.stack([blocks[:, 1], blocks[:, 3]]), 1), 1)
            away, blocks = step((away, blocks))
            near = [blocks[:, 2 * k].astype(F32) + away[k].astype(F32) for k in range(2)]
            by_row = self.hop(self.turn(near[1][:, :half].astype(BF), 2), 2)
            far = jnp.stack([near[0][1, half:], near[1][1, half:]]).astype(BF)
            by_col = self.hop(far, 0, 1)
            by_row, by_col, near = step((by_row, by_col, near))
            first = [near[0][k, :half] + by_row[k].astype(F32) for k in range(2)]
            second = [near[k][0, half:] + by_col[k].astype(F32) for k in range(2)]
            last_col = self.hop(first[1].astype(BF), 0, 1).astype(F32)
            last_row = self.hop(self.turn(second[1].astype(BF), 2), 2).astype(F32)
            return step(jnp.concatenate([first[0] + last_col, second[0] + last_row], axis=0))
        sums = {}
        for col_xor in reversed(range(self.cols)):
            for row_xor in reversed(range(0, self.rows, 2)):
                arrived = self.hop(self.turn(blocks[col_xor, row_xor + 1], 1), 1)
                sums[col_xor, row_xor] = blocks[col_xor, row_xor].astype(F32) + arrived.astype(F32)
        total = sums[0, 0]
        for col_xor in reversed(range(self.cols)):
            for row_xor in reversed(range(0, self.rows, 2)):
                if col_xor or row_xor:
                    sent = self.turn(sums[col_xor, row_xor].astype(BF), row_xor)
                    total = total + self.hop(sent, row_xor, col_xor).astype(F32)
        return total

    def total(self, array):
        blocks = array.reshape(array.shape[:-1] + (self.cols, self.rows, -1))
        row_xor = 1
        while row_xor < self.rows:
            order = [index ^ row_xor for index in range(self.rows)]
            arrived = self.hop(blocks, row_xor)
            blocks = blocks + jnp.stack([arrived[..., k, :] for k in order], axis=-2)
            row_xor *= 2
        col_xor = 1
        while col_xor < self.cols:
            order = [index ^ col_xor for index in range(self.cols)]
            arrived = self.hop(blocks, 0, col_xor)
            blocks = blocks + jnp.stack([arrived[..., k, :, :] for k in order], axis=-3)
            col_xor *= 2
        return blocks.reshape(array.shape)


ENDS = [(0, 1), (1, 0), (2, 3), (3, 2)]
MIDDLE = [(1, 2), (2, 1)]


def plus(one, other):
    return (one.astype(F32) + other.astype(F32)).astype(BF)


class Line:
    depth = 2

    def __init__(self, move):
        self.move = move
        self.line = lax.axis_size("dp") == 4
        place = lax.axis_index("dp")
        self.inner = (place == 1) | (place == 2)
        self.arrays, self.pairs, self.full, self.placed = [], [], [], []
        self.pending = [{}] * self.depth
        self.moving = [[]] * (self.depth + 1)
        self.sent_back = 0

    def step(self, values, array=None):
        if not self.line:
            if array is not None:
                self.arrays.append(array)
            return values
        pending, moving, array, values = together(
            self.pending.pop(0), self.moving.pop(0), array, values
        )
        self.advance(pending, moving, array)
        return values

    def advance(self, pending, moving, array):
        self.placed += moving
        current, moved = {}, []
        if "back" in pending:
            total = jnp.where(self.inner, pending["full"], pending["back"])
            moved.append(self.move(len(self.placed) + sum(map(len, self.moving)), total))
        self.moving.append(moved)
        if "across" in pending:
            self.full.append(plus(self.pairs[len(self.full)], pending["across"]))
        if "inward" in pending:
            pair = plus(self.arrays[len(self.pairs)], pending["inward"])
            self.pairs.append(pair)
            current["across"] = lax.ppermute(pair, "dp", MIDDLE)
        back = None
        if len(self.full) > self.sent_back:
            back = self.full[self.sent_back]
            self.sent_back += 1
        if array is not None:
            self.arrays.append(array)
        if back is not None and array is not None and back.shape == array.shape:
            sent = jnp.where(self.inner, back, array)
            current["full"] = sent
            current["inward"] = lax.ppermute(sent, "dp", ENDS)
            current["back"] = current["inward"]
        else:
            if array is not None:
                current["inward"] = lax.ppermute(array, "dp", [(0, 1), (3, 2)])
            if back is not None:
                current["full"] = back
                current["back"] = lax.ppermute(back, "dp", [(1, 0), (2, 3)])
        self.pending.append(current)

    def finish(self):
        if not self.line:
            totals = [lax.psum(array, "dp") for array in self.arrays]
            return [self.move(index, total) for index, total in enumerate(totals)]
        while len(self.placed) < len(self.arrays):
            self.advance(self.pending.pop(0), self.moving.pop(0), None)
        return self.placed


def shards(
    layer_input,
    cotangent,
    lengths,
    deal_slot,
    query_weight,
    key_weight,
    value_weight,
    out_weight,
    query_gain,
    key_gain,
    attn_gain,
    gate_weight,
    up_weight,
    down_weight,
    mlp_gain,
):
    groups = lax.axis_size("dp")
    my_group = lax.axis_index("dp")
    seq_grp, tok_seq, width = layer_input.shape
    seq_count = lengths.shape[0]
    plane = Plane(width)
    rows, cols, row, col, part = plane.rows, plane.cols, plane.row, plane.col, plane.part
    seq_own = seq_grp // cols
    tok_own = seq_own * tok_seq
    seq_len = tok_seq * rows
    tok_all = seq_grp * seq_len
    heads_cols = query_weight.shape[1]
    head_part = heads_cols // rows
    heads_here = head_part // HD
    ff_part = gate_weight.shape[1] // rows

    first_own = col * seq_own
    all_input = plane.relative(layer_input)
    own_cot = plane.relative(
        lax.dynamic_slice_in_dim(cotangent, first_own, seq_own, axis=0).reshape(tok_own, width)
    )
    own_places = row * tok_seq + jnp.arange(tok_seq, dtype=jnp.int32)
    group_len = lax.dynamic_slice_in_dim(lengths, my_group * seq_grp, seq_grp)
    valid_all = (own_places[None, :] < group_len[:, None]).astype(BF)
    all_input = (all_input * valid_all[:, :, None]).reshape(cols, tok_own, width)
    all_input = jnp.stack(
        [
            lax.dynamic_index_in_dim(all_input, col ^ index, axis=0, keepdims=False)
            for index in range(cols)
        ]
    )
    inputs_low = all_input[0]
    own_len = lax.dynamic_slice_in_dim(lengths, my_group * seq_grp + first_own, seq_own)
    valid_rows = (own_places[None, :] < own_len[:, None]).astype(F32).reshape(tok_own, 1)
    inputs = inputs_low.astype(F32)
    d_full = own_cot.astype(F32) * valid_rows
    inputs_all = plane.gather_columns(all_input)

    def pieces_of(weight, axis):
        size = weight.shape[axis] // rows
        return [
            lax.dynamic_slice_in_dim(weight, (row ^ k) * size, size, axis=axis)
            for k in range(rows)
        ]

    def shared(weight, axis):
        pieces = pieces_of(weight, axis)
        size = pieces[0].shape[0] // groups
        parts = [
            plane.hop(lax.dynamic_slice_in_dim(piece, my_group * size, size, axis=0), k)
            for k, piece in enumerate(pieces)
            if k >= 2
        ]
        return pieces[:1] + [plane.hop(pieces[1], 1)], jnp.concatenate(parts, axis=1)

    def whole(pieces, far, axis):
        return jnp.concatenate(pieces + jnp.split(far, rows - 2, axis=1), axis=axis)

    def over_groups(part):
        return lax.all_gather(part, "dp", axis=0, tiled=True)

    gate_pieces, gate_far = shared(gate_weight, 1)
    trios = [
        jnp.stack(trio)
        for trio in zip(
            pieces_of(query_weight, 1),
            pieces_of(key_weight, 1),
            pieces_of(value_weight, 1),
            strict=True,
        )
    ]
    gate_far, trios[2:] = together(gate_far, trios[2:])
    gate_far = over_groups(gate_far)
    trios = [plane.hop(trio, k) for k, trio in enumerate(trios)]
    gate_far, trios, inputs_all = together(gate_far, trios, inputs_all)
    up_pieces, up_far = shared(up_weight, 1)
    down_pieces = pieces_of(down_weight, 0)
    w_query, w_key, w_value = (
        jnp.concatenate([trio[k] for trio in trios], axis=0) for k in range(3)
    )
    out_pieces = [plane.hop(piece, k) for k, piece in enumerate(pieces_of(out_weight, 0))]
    gains = jnp.stack([attn_gain, mlp_gain])
    gains = jnp.concatenate([plane.hop(gains, k) for k in range(rows)], axis=1).astype(F32)
    attn_gain_f, mlp_gain_f = gains[0:1], gains[1:2]
    q_gain_f = lax.dynamic_slice_in_dim(query_gain, row * head_part, head_part).astype(F32)
    k_gain_f = lax.dynamic_slice_in_dim(key_gain, row * head_part, head_part).astype(F32)

    def by_sequence(array):
        shape = (cols, rows, seq_own, tok_seq) + array.shape[1:]
        return jnp.swapaxes(array.reshape(shape), 1, 2).reshape(
            (seq_grp, seq_len) + array.shape[1:]
        )

    def by_block(array):
        shape = (cols, seq_own, rows, tok_seq) + array.shape[2:]
        return jnp.swapaxes(array.reshape(shape), 1, 2).reshape((tok_all,) + array.shape[2:])

    query_raw = dot(inputs_all, w_query)
    key_raw = dot(inputs_all, w_key)
    value_low = dot(inputs_all, w_value).astype(BF)
    squares = jnp.stack(
        [jnp.sum(query_raw * query_raw, axis=1), jnp.sum(key_raw * key_raw, axis=1)]
    )
    scales = lax.rsqrt(plane.total(squares) / width + EPSILON)
    q_scale = scales[0][:, None]
    k_scale = scales[1][:, None]
    q_unit = query_raw * q_scale
    k_unit = key_raw * k_scale
    block_rows = row ^ jnp.arange(rows, dtype=jnp.int32)
    places = (
        block_rows[:, None] * tok_seq + jnp.arange(tok_seq, dtype=jnp.int32)[None, :]
    ).reshape(seq_len)
    block_cols = col ^ jnp.arange(cols, dtype=jnp.int32)
    seq_ids = (
        my_group * seq_grp
        + block_cols[:, None] * seq_own
        + jnp.arange(seq_own, dtype=jnp.int32)[None, :]
    ).reshape(seq_grp)
    live_len = jnp.sum(
        jnp.where(
            seq_ids[:, None] == jnp.arange(seq_count, dtype=jnp.int32)[None, :], lengths[None, :], 0
        ),
        axis=1,
    )
    frequency = ROPE_THETA ** (-(jnp.arange(HD // 2).astype(F32) * 2.0 / HD))
    angles = places.astype(F32)[:, None] * frequency[None, :]
    cos_table = jnp.cos(angles)[None, :, None, :]
    sin_table = jnp.sin(angles)[None, :, None, :]
    head_shape = (seq_grp, seq_len, heads_here, HD)

    def heads_of(array):
        return by_sequence(array).reshape(head_shape)

    def joined(array):
        return by_block(array.reshape(seq_grp, seq_len, head_part))

    q_rot = rotate_pairs(heads_of(q_unit * q_gain_f), cos_table, sin_table).astype(BF)
    k_rot = rotate_pairs(heads_of(k_unit * k_gain_f), cos_table, sin_table).astype(BF)
    values = heads_of(value_low)
    down_half = rows // 2
    out_pieces, down_pieces = together(out_pieces, down_pieces)
    down_pieces = [plane.hop(piece, k) for k, piece in enumerate(down_pieces)]
    up_far, down_pieces[: down_half + 1], q_rot = together(
        up_far, down_pieces[: down_half + 1], q_rot
    )
    w_out = jnp.concatenate(out_pieces, axis=1)
    up_far = over_groups(up_far)
    allowed = (places[None, None, :] <= places[None, :, None]) & (
        places[None, None, :] < live_len[:, None, None]
    )
    score_scale = HD ** (-0.5)
    scores = (
        jnp.einsum("sqhd,skhd->shqk", q_rot, k_rot, preferred_element_type=F32) * score_scale
    )
    scores = jnp.where(allowed[:, None], scores, -MASK_VALUE)
    exponent = jnp.exp(scores - jnp.max(scores, axis=-1, keepdims=True))
    prob = exponent / jnp.sum(exponent, axis=-1, keepdims=True)
    prob_low = prob.astype(BF)
    attn_mix = joined(
        jnp.einsum("shqk,skhd->sqhd", prob_low, values, preferred_element_type=F32).astype(BF)
    )
    up_far, down_pieces, attn_mix = together(up_far, down_pieces, attn_mix)
    attn_raw = plane.scatter(dot(attn_mix, w_out).astype(BF))
    w_gate = whole(gate_pieces, gate_far, 0)
    w_up = whole(up_pieces, up_far, 0)
    w_down = jnp.concatenate(down_pieces, axis=1)
    a_scale = rms_scale(attn_raw)
    a_unit = attn_raw * a_scale
    branch_a = a_unit * attn_gain_f
    hidden = inputs + branch_a
    hidden_all = plane.gather(hidden.astype(BF))
    gate_pre = dot(hidden_all, w_gate)
    up_pre = dot(hidden_all, w_up)
    gate_sig = jax.nn.sigmoid(gate_pre)
    gate_act = gate_pre * gate_sig
    inner_low = (gate_act * up_pre).astype(BF)
    mlp_raw = plane.scatter(dot(inner_low, w_down).astype(BF))
    m_scale = rms_scale(mlp_raw)
    m_unit = mlp_raw * m_scale
    branch_m = m_unit * mlp_gain_f
    result = (hidden + branch_m) * valid_rows

    d_m_unit = d_full * mlp_gain_f
    d_mlp = m_scale * (d_m_unit - m_unit * jnp.mean(d_m_unit * m_unit, axis=-1, keepdims=True))
    d_mlp_all = plane.gather(d_mlp.astype(BF))
    order = list(range(rows // 2, rows)) + list(range(rows // 2))
    near, far = slice(0, width // 2), slice(width // 2, width)
    low, high = slice(0, ff_part // 2), slice(ff_part // 2, ff_part)
    waiting = []

    def move(index, total):
        if index < 4:
            first = rows // 2 if index < 2 else 0
            blocks = jnp.split(total, rows // 2, axis=1)
            return [plane.hop(block, first + k) for k, block in enumerate(blocks)]
        if index == 3 + 3 * rows:
            return plane.hop(total[:part], order[-1]), total[part:]
        return plane.hop(total, order[index % rows])

    line = Line(move)

    def outer(left_side, right_side):
        return against(left_side, right_side).astype(BF)

    def step(values):
        return line.step(values, waiting.pop(0) if waiting else None)

    waiting += [outer(inner_low[:, low], d_mlp_all[:, far])]
    d_mlp_all = step(d_mlp_all)
    waiting += [outer(inner_low[:, high], d_mlp_all[:, far])]
    waiting += [outer(inner_low[:, half], d_mlp_all[:, near]) for half in (low, high)]
    d_inner = through(d_mlp_all, w_down)
    d_gate_low = (d_inner * up_pre * (gate_sig * (1.0 + gate_pre * (1.0 - gate_sig)))).astype(BF)
    d_up_low = (d_inner * gate_act).astype(BF)
    d_gate_low, d_up_low = step((d_gate_low, d_up_low))
    waiting += [outer(plane.slot(hidden_all, k), d_gate_low) for k in order]
    waiting += [outer(plane.slot(hidden_all, k), d_up_low) for k in order]
    partial = step((through(d_gate_low, w_gate) + through(d_up_low, w_up)).astype(BF))
    d_hidden = d_full + plane.scatter(partial, step)
    d_a_unit = d_hidden * attn_gain_f
    d_attn = a_scale * (d_a_unit - a_unit * jnp.mean(d_a_unit * a_unit, axis=-1, keepdims=True))
    d_attn_all = plane.gather(d_attn.astype(BF), step)
    d_mix = heads_of(through(d_attn_all, w_out).astype(BF))
    d_prob = jnp.einsum("sqhd,skhd->shqk", d_mix, values, preferred_element_type=F32)
    row_delta = jnp.sum(prob * d_prob, axis=-1, keepdims=True)
    d_scores = step((prob * (d_prob - row_delta)).astype(BF))
    d_qrot = (
        jnp.einsum("shqk,skhd->sqhd", d_scores, k_rot, preferred_element_type=F32) * score_scale
    )
    d_krot = (
        jnp.einsum("shqk,sqhd->skhd", d_scores, q_rot, preferred_element_type=F32) * score_scale
    )
    d_value = jnp.einsum("shqk,sqhd->skhd", prob_low, d_mix, preferred_element_type=F32)
    d_qn = joined(rotate_pairs(d_qrot, cos_table, -sin_table))
    d_kn = joined(rotate_pairs(d_krot, cos_table, -sin_table))
    d_value = joined(d_value.astype(BF))
    d_q_hat = d_qn * q_gain_f
    d_k_hat = d_kn * k_gain_f
    d_q_hat, d_k_hat, d_value = step((d_q_hat, d_k_hat, d_value))
    inners = plane.total(
        jnp.stack([jnp.sum(d_q_hat * q_unit, axis=1), jnp.sum(d_k_hat * k_unit, axis=1)])
    )
    inners = step(inners)
    d_query = q_scale * (d_q_hat - q_unit * (inners[0] / width)[:, None])
    d_key = k_scale * (d_k_hat - k_unit * (inners[1] / width)[:, None])
    d_query = d_query.astype(BF)
    d_key = d_key.astype(BF)
    d_qkv = jnp.concatenate([d_query, d_key, d_value], axis=1)
    waiting += [
        jnp.concatenate(
            [
                outer(plane.slot(inputs_all, k), d_qkv),
                outer(plane.slot(d_attn_all, k), attn_mix),
            ],
            axis=1,
        )
        for k in order
    ]
    partial = step(
        (through(d_query, w_query) + through(d_key, w_key) + through(d_value, w_value)).astype(BF)
    )
    d_inputs = d_hidden + plane.scatter(partial)
    while len(waiting) > 1:
        step(())
    line.placed, d_inputs, result_late = together(line.placed, d_inputs, result)

    def home(array):
        own = plane.relative((array).astype(BF)).reshape(seq_own, tok_seq, width)
        pieces = [own] + [plane.hop(own, 0, k) for k in range(1, cols)]
        out = jnp.zeros((seq_grp, tok_seq, width), BF)
        for k in range(cols):
            out = lax.dynamic_update_slice_in_dim(out, pieces[k], (col ^ k) * seq_own, axis=0)
        return out

    output = home(result_late)
    grad_input = home(d_inputs * valid_rows)

    def sums_of(array):
        return jnp.sum(array.reshape(seq_own, tok_seq * width), axis=1)

    own_sums = jnp.stack(
        [
            sums_of(result * result),
            sums_of(branch_a * branch_a * valid_rows),
            sums_of(branch_m * branch_m * valid_rows),
        ],
        axis=1,
    )
    own_ids = my_group * seq_grp + first_own + jnp.arange(seq_own, dtype=jnp.int32)
    seq_sums = jnp.sum(
        jnp.where(
            own_ids[:, None, None] == jnp.arange(seq_count, dtype=jnp.int32)[None, :, None],
            own_sums[:, None, :],
            0.0,
        ),
        axis=0,
    )
    gain_sums = plane.relative(
        jnp.stack([jnp.sum(d_hidden * a_unit, axis=0), jnp.sum(d_full * m_unit, axis=0)])
    )
    head_sums = jnp.stack([jnp.sum(d_qn * q_unit, axis=0), jnp.sum(d_kn * k_unit, axis=0)])
    mine = (
        (jnp.arange(cols)[:, None] == col) & (jnp.arange(rows)[None, :] == row)
    ).astype(F32)
    head_sums = (head_sums[:, None, None, :] * mine[None, :, :, None]).reshape(2, cols, heads_cols)
    vector = jnp.concatenate([gain_sums.reshape(-1), head_sums.reshape(-1), seq_sums.reshape(-1)])
    vector = jnp.pad(vector, (0, -vector.shape[0] % (ff_part * 16))).reshape(-1, ff_part)
    row_xor = 1
    while row_xor < rows:
        vector = vector + plane.hop(vector, row_xor)
        row_xor *= 2
    col_xor = 1
    while col_xor < cols:
        vector = vector + plane.hop(vector, 0, col_xor)
        col_xor *= 2

    def finish(blocks, axis):
        size = blocks[0].shape[axis]
        shape = list(blocks[0].shape)
        shape[axis] = size * rows
        out = jnp.zeros(shape, F32)
        for k in reversed(range(rows)):
            start = [0, 0]
            start[axis] = (row ^ k) * size
            out = lax.dynamic_update_slice(out, blocks[k].astype(F32), start)
        return out

    def arrived_at(placed):
        return [placed[order.index(k)] for k in range(rows)]

    line.step((), jnp.concatenate([waiting.pop(0), vector.astype(BF)], axis=0))
    placed = line.finish()
    placed[-1], vector = placed[-1]
    vector = vector.astype(F32).reshape(-1)
    grad_down = [placed[2] + placed[0], placed[3] + placed[1]]
    grad_down = finish([jnp.concatenate(both, axis=0) for both in zip(*grad_down, strict=True)], 0)
    grad_gate = finish(arrived_at(placed[4 : 4 + rows]), 1)
    grad_up = finish(arrived_at(placed[4 + rows : 4 + 2 * rows]), 1)
    attn_blocks = arrived_at(placed[4 + 2 * rows :])
    grad_query, grad_key, grad_value, grad_out = (
        [block[:, k * head_part : (k + 1) * head_part] for block in attn_blocks] for k in range(4)
    )
    grad_query, grad_key, grad_value = (
        finish(blocks, 1) for blocks in (grad_query, grad_key, grad_value)
    )
    grad_out = finish([block.T for block in grad_out], 0)

    gain_sums = lax.dynamic_slice_in_dim(
        vector[: 2 * width].reshape(2, width), row * part, part, axis=1
    )
    head_end = 2 * width + 2 * cols * heads_cols
    head_sums = lax.dynamic_slice_in_dim(
        vector[2 * width : head_end].reshape(2, cols, heads_cols), col, 1, axis=1
    )
    seq_sums = vector[head_end : head_end + 3 * seq_count].reshape(seq_count, 3)
    member = (
        (deal_slot // seq_grp)[:, None] == jnp.arange(groups, dtype=jnp.int32)[None, :]
    ).astype(F32)
    counts = jnp.sum(member * lengths.astype(F32)[:, None], axis=0)
    stat_sums = jnp.sum(member[:, :, None] * seq_sums[:, None, :], axis=0)
    rms_stats = jnp.sqrt(stat_sums / (counts[:, None] * width))
    return (
        output,
        grad_input,
        grad_query,
        grad_key,
        grad_value,
        grad_out,
        head_sums[0, 0],
        head_sums[1, 0],
        gain_sums[0],
        grad_gate,
        grad_up,
        grad_down,
        gain_sums[1],
        rms_stats,
    )


def solution(mesh):
    tokens = P("dp", "row", None)
    inward = P("row", "col")
    outward = P("col", "row")
    in_specs = (
        (tokens, tokens, P(), P())
        + (inward, inward, inward, outward)
        + (P("col"), P("col"), P("row"))
        + (inward, inward, outward, P("row"))
    )
    out_specs = (
        (tokens, tokens)
        + (inward, inward, inward, outward)
        + (P("col"), P("col"), P("row"))
        + (inward, inward, outward, P("row"))
        + (P(),)
    )
    return jax.shard_map(shards, mesh=mesh, in_specs=in_specs, out_specs=out_specs, check_vma=False)
```

```python
import jax
import jax.numpy as jnp
from jax import lax
from jax.experimental import pallas as pl
from jax.experimental.pallas import tpu as pltpu
from jax.sharding import PartitionSpec as P

HD = 128
EPSILON = 1e-06
ROPE_THETA = 500000.0
MASK_VALUE = 1e30
BF = jnp.bfloat16
F32 = jnp.float32


def rms_scale(matrix):
    return lax.rsqrt(jnp.mean(matrix * matrix, axis=-1, keepdims=True) + EPSILON)


def masked_prob(length, q_rot, k_rot, place_col, place_row):
    scores = through(q_rot, k_rot) * HD ** (-0.5)
    allowed = (place_row <= place_col) & (place_row < length)
    scores = jnp.where(allowed, scores, -MASK_VALUE)
    exponent = jnp.exp(scores - jnp.max(scores, axis=-1, keepdims=True))
    return exponent / jnp.sum(exponent, axis=-1, keepdims=True)


def attend_kernel(
    length, query, key, value, cos, sin, place_col, place_row, mix, q_out, k_out
):
    def turned(normed):
        normed = normed[...]
        return (normed * cos[...] + pltpu.roll(normed, HD // 2, 1) * sin[...]).astype(BF)

    q_rot, k_rot = turned(query), turned(key)
    q_out[...], k_out[...] = q_rot, k_rot
    prob = masked_prob(length[pl.program_id(0)], q_rot, k_rot, place_col[...], place_row[...])
    mix[...] = dot(prob.astype(BF), value[...]).astype(BF)


def attend_back_kernel(
    length, q_rot, k_rot, value, d_mix, cos, sin, place_col, place_row, d_query, d_key, d_value
):
    q_rot, k_rot, d_mix = q_rot[...], k_rot[...], d_mix[...]
    prob = masked_prob(length[pl.program_id(0)], q_rot, k_rot, place_col[...], place_row[...])
    d_value[...] = against(prob.astype(BF), d_mix).astype(BF)
    d_prob = through(d_mix, value[...])
    row_delta = jnp.sum(prob * d_prob, axis=-1, keepdims=True)
    d_scores = (prob * (d_prob - row_delta)).astype(BF)

    def turned_back(grad):
        grad = grad * HD ** (-0.5)
        return grad * cos[...] - pltpu.roll(grad, HD // 2, 1) * sin[...]

    d_query[...] = turned_back(dot(d_scores, k_rot))
    d_key[...] = turned_back(against(d_scores, q_rot))


def over_heads(kernel, lengths, seq_len, outs, *arrays):
    tokens, features = arrays[0].shape

    def spec(shape):
        if shape == (tokens, features):
            return pl.BlockSpec((seq_len, HD), lambda s, h, *_: (s, h))
        return pl.BlockSpec(shape, lambda s, h, *_: (0, 0))

    count = tokens * features // HD
    return pl.pallas_call(
        kernel,
        out_shape=tuple(jax.ShapeDtypeStruct((tokens, features), dtype) for dtype in outs),
        grid_spec=pltpu.PrefetchScalarGridSpec(
            num_scalar_prefetch=1,
            grid=(tokens // seq_len, features // HD),
            in_specs=[spec(array.shape) for array in arrays],
            out_specs=tuple(spec((tokens, features)) for _ in outs),
        ),
        cost_estimate=pl.CostEstimate(
            flops=4 * len(outs) * count * seq_len * HD,
            bytes_accessed=4 * (len(arrays) + len(outs)) * tokens * features,
            transcendentals=count * seq_len,
        ),
    )(lengths, *arrays)


def dot(left_side, right_side):
    return jnp.dot(left_side, right_side, preferred_element_type=F32)


def against(left_side, right_side):
    return lax.dot_general(
        left_side, right_side, (((0,), (0,)), ((), ())), preferred_element_type=F32
    )


def through(left_side, weight):
    return lax.dot_general(
        left_side, weight, (((1,), (1,)), ((), ())), preferred_element_type=F32
    )


def together(*values):
    return lax.optimization_barrier(values)


def unchanged(value):
    return value


class Plane:
    def __init__(self, width):
        self.rows = lax.axis_size("row")
        self.cols = lax.axis_size("col")
        self.row = lax.axis_index("row")
        self.col = lax.axis_index("col")
        self.part = width // self.rows

    def hop(self, array, row_xor, col_xor=0):
        if row_xor and col_xor:
            pairs = [
                (a * self.cols + b, (a ^ row_xor) * self.cols + (b ^ col_xor))
                for a in range(self.rows)
                for b in range(self.cols)
            ]
            return lax.ppermute(array, ("row", "col"), pairs)
        if row_xor:
            return lax.ppermute(array, "row", [(a, a ^ row_xor) for a in range(self.rows)])
        if col_xor:
            return lax.ppermute(array, "col", [(a, a ^ col_xor) for a in range(self.cols)])
        return array

    def slot(self, array, index):
        return array[..., index * self.part : (index + 1) * self.part]

    def turn(self, array, row_xor):
        if row_xor == 0:
            return array
        return jnp.concatenate(
            [self.slot(array, index ^ row_xor) for index in range(self.rows)], axis=-1
        )

    def relative(self, array):
        return jnp.concatenate(
            [
                lax.dynamic_slice_in_dim(
                    array, (self.row ^ index) * self.part, self.part, axis=array.ndim - 1
                )
                for index in range(self.rows)
            ],
            axis=-1,
        )

    def gather(self, own, step=unchanged):
        blocks = {(0, 0): own}
        if self.rows == 4 and self.cols == 2:
            half = own.shape[0] // 2
            blocks[0, 2] = self.hop(self.turn(own, 2), 2)
            blocks[1, 0] = self.hop(own, 0, 1)
            blocks = step(blocks)
            blocks[1, 2] = jnp.concatenate(
                [
                    self.hop(blocks[0, 2][:half], 0, 1),
                    self.hop(self.turn(blocks[1, 0][half:], 2), 2),
                ],
                axis=0,
            )
        else:
            for col_xor in reversed(range(self.cols)):
                for row_xor in reversed(range(0, self.rows, 2)):
                    blocks[col_xor, row_xor] = self.hop(self.turn(own, row_xor), row_xor, col_xor)
        return step(self.over_cores(blocks))

    def over_cores(self, blocks):
        for col_xor in range(self.cols):
            for row_xor in range(0, self.rows, 2):
                blocks[col_xor, row_xor + 1] = self.hop(
                    self.turn(blocks[col_xor, row_xor], 1), 1
                )
        return jnp.concatenate(
            [blocks[b, a] for b in range(self.cols) for a in range(self.rows)], axis=0
        )

    def gather_columns(self, own):
        blocks = {}
        for row_xor in range(0, self.rows, 2):
            arrived = self.hop(self.turn(own[0], row_xor), row_xor)
            for col_xor in range(self.cols):
                if row_xor:
                    blocks[col_xor, row_xor] = self.hop(arrived, 0, col_xor)
                else:
                    blocks[col_xor, row_xor] = own[col_xor]
        return self.over_cores(blocks)

    def scatter(self, partial, step=unchanged):
        tokens = partial.shape[0] // (self.rows * self.cols)
        blocks = partial.reshape(self.cols, self.rows, tokens, -1)
        if self.rows == 4 and self.cols == 2:
            half = tokens // 2
            away = self.hop(self.turn(jnp.stack([blocks[:, 1], blocks[:, 3]]), 1), 1)
            away, blocks = step((away, blocks))
            near = [blocks[:, 2 * k].astype(F32) + away[k].astype(F32) for k in range(2)]
            by_row = self.hop(self.turn(near[1][:, :half].astype(BF), 2), 2)
            far = jnp.stack([near[0][1, half:], near[1][1, half:]]).astype(BF)
            by_col = self.hop(far, 0, 1)
            by_row, by_col, near = step((by_row, by_col, near))
            first = [near[0][k, :half] + by_row[k].astype(F32) for k in range(2)]
            second = [near[k][0, half:] + by_col[k].astype(F32) for k in range(2)]
            last_col = self.hop(first[1].astype(BF), 0, 1).astype(F32)
            last_row = self.hop(self.turn(second[1].astype(BF), 2), 2).astype(F32)
            return step(jnp.concatenate([first[0] + last_col, second[0] + last_row], axis=0))
        sums = {}
        for col_xor in reversed(range(self.cols)):
            for row_xor in reversed(range(0, self.rows, 2)):
                arrived = self.hop(self.turn(blocks[col_xor, row_xor + 1], 1), 1)
                sums[col_xor, row_xor] = blocks[col_xor, row_xor].astype(F32) + arrived.astype(F32)
        total = sums[0, 0]
        for col_xor in reversed(range(self.cols)):
            for row_xor in reversed(range(0, self.rows, 2)):
                if col_xor or row_xor:
                    sent = self.turn(sums[col_xor, row_xor].astype(BF), row_xor)
                    total = total + self.hop(sent, row_xor, col_xor).astype(F32)
        return total

    def total(self, array):
        blocks = array.reshape(array.shape[:-1] + (self.cols, self.rows, -1))
        row_xor = 1
        while row_xor < self.rows:
            order = [index ^ row_xor for index in range(self.rows)]
            arrived = self.hop(blocks, row_xor)
            blocks = blocks + jnp.stack([arrived[..., k, :] for k in order], axis=-2)
            row_xor *= 2
        col_xor = 1
        while col_xor < self.cols:
            order = [index ^ col_xor for index in range(self.cols)]
            arrived = self.hop(blocks, 0, col_xor)
            blocks = blocks + jnp.stack([arrived[..., k, :, :] for k in order], axis=-3)
            col_xor *= 2
        return blocks.reshape(array.shape)


ENDS = [(0, 1), (1, 0), (2, 3), (3, 2)]
MIDDLE = [(1, 2), (2, 1)]


def plus(one, other):
    return (one.astype(F32) + other.astype(F32)).astype(BF)


class Line:
    depth = 2

    def __init__(self, move):
        self.move = move
        self.line = lax.axis_size("dp") == 4
        place = lax.axis_index("dp")
        self.inner = (place == 1) | (place == 2)
        self.arrays, self.pairs, self.full, self.placed = [], [], [], []
        self.pending = [{}] * self.depth
        self.moving = [[]] * (self.depth + 1)
        self.sent_back = 0

    def step(self, values, array=None):
        if not self.line:
            if array is not None:
                self.arrays.append(array)
            return values
        if 0 < len(self.arrays) <= self.depth + 2:
            last = self.pending[-1]
            last["inward"], array = together(last["inward"], array)
        pending, moving, array, values = together(
            self.pending.pop(0), self.moving.pop(0), array, values
        )
        self.advance(pending, moving, array)
        return values

    def advance(self, pending, moving, array):
        self.placed += moving
        current, moved = {}, []
        if "back" in pending:
            total = jnp.where(self.inner, pending["full"], pending["back"])
            moved.append(self.move(len(self.placed) + sum(map(len, self.moving)), total))
        self.moving.append(moved)
        if "across" in pending:
            self.full.append(plus(self.pairs[len(self.full)], pending["across"]))
        if "inward" in pending:
            pair = plus(self.arrays[len(self.pairs)], pending["inward"])
            self.pairs.append(pair)
            current["across"] = lax.ppermute(pair, "dp", MIDDLE)
        back = None
        if len(self.full) > self.sent_back:
            back = self.full[self.sent_back]
            self.sent_back += 1
        if array is not None:
            self.arrays.append(array)
        if back is not None and array is not None and back.shape == array.shape:
            sent = jnp.where(self.inner, back, array)
            current["full"] = sent
            current["inward"] = lax.ppermute(sent, "dp", ENDS)
            current["back"] = current["inward"]
        else:
            if array is not None:
                current["inward"] = lax.ppermute(array, "dp", [(0, 1), (3, 2)])
            if back is not None:
                current["full"] = back
                current["back"] = lax.ppermute(back, "dp", [(1, 0), (2, 3)])
        self.pending.append(current)

    def finish(self):
        if not self.line:
            totals = [lax.psum(array, "dp") for array in self.arrays]
            return [self.move(index, total) for index, total in enumerate(totals)]
        while len(self.placed) < len(self.arrays):
            self.advance(self.pending.pop(0), self.moving.pop(0), None)
        return self.placed


def shards(
    layer_input,
    cotangent,
    lengths,
    deal_slot,
    query_weight,
    key_weight,
    value_weight,
    out_weight,
    query_gain,
    key_gain,
    attn_gain,
    gate_weight,
    up_weight,
    down_weight,
    mlp_gain,
):
    groups = lax.axis_size("dp")
    my_group = lax.axis_index("dp")
    seq_grp, tok_seq, width = layer_input.shape
    seq_count = lengths.shape[0]
    plane = Plane(width)
    rows, cols, row, col, part = plane.rows, plane.cols, plane.row, plane.col, plane.part
    seq_own = seq_grp // cols
    tok_own = seq_own * tok_seq
    seq_len = tok_seq * rows
    tok_all = seq_grp * seq_len
    heads_cols = query_weight.shape[1]
    head_part = heads_cols // rows
    ff_part = gate_weight.shape[1] // rows

    first_own = col * seq_own
    all_input = plane.relative(layer_input)
    own_cot = plane.relative(
        lax.dynamic_slice_in_dim(cotangent, first_own, seq_own, axis=0).reshape(tok_own, width)
    )
    own_places = row * tok_seq + jnp.arange(tok_seq, dtype=jnp.int32)
    group_len = lax.dynamic_slice_in_dim(lengths, my_group * seq_grp, seq_grp)
    valid_all = (own_places[None, :] < group_len[:, None]).astype(BF)
    all_input = (all_input * valid_all[:, :, None]).reshape(cols, tok_own, width)
    all_input = jnp.stack(
        [
            lax.dynamic_index_in_dim(all_input, col ^ index, axis=0, keepdims=False)
            for index in range(cols)
        ]
    )
    inputs_low = all_input[0]
    own_len = lax.dynamic_slice_in_dim(lengths, my_group * seq_grp + first_own, seq_own)
    valid_rows = (own_places[None, :] < own_len[:, None]).astype(F32).reshape(tok_own, 1)
    inputs = inputs_low.astype(F32)
    d_full = own_cot.astype(F32) * valid_rows
    inputs_all = plane.gather_columns(all_input)

    def pieces_of(weight, axis):
        size = weight.shape[axis] // rows
        return [
            lax.dynamic_slice_in_dim(weight, (row ^ k) * size, size, axis=axis)
            for k in range(rows)
        ]

    def shared(weight, axis):
        pieces = pieces_of(weight, axis)
        size = pieces[0].shape[0] // groups
        parts = [
            plane.hop(lax.dynamic_slice_in_dim(piece, my_group * size, size, axis=0), k)
            for k, piece in enumerate(pieces)
            if k >= 2
        ]
        return pieces[:1] + [plane.hop(pieces[1], 1)], jnp.concatenate(parts, axis=1)

    def whole(pieces, far, axis):
        return jnp.concatenate(pieces + jnp.split(far, rows - 2, axis=1), axis=axis)

    def over_groups(part):
        return lax.all_gather(part, "dp", axis=0, tiled=True)

    gate_pieces, gate_far = shared(gate_weight, 1)
    trios = [
        jnp.stack(trio)
        for trio in zip(
            pieces_of(query_weight, 1),
            pieces_of(key_weight, 1),
            pieces_of(value_weight, 1),
            strict=True,
        )
    ]
    gate_far, trios[2:] = together(gate_far, trios[2:])
    gate_far = over_groups(gate_far)
    trios = [plane.hop(trio, k) for k, trio in enumerate(trios)]
    gate_far, trios, inputs_all = together(gate_far, trios, inputs_all)
    up_pieces, up_far = shared(up_weight, 1)
    down_pieces = pieces_of(down_weight, 0)
    w_query, w_key, w_value = (
        jnp.concatenate([trio[k] for trio in trios], axis=0) for k in range(3)
    )
    out_pieces = [plane.hop(piece, k) for k, piece in enumerate(pieces_of(out_weight, 0))]
    gains = jnp.stack([attn_gain, mlp_gain])
    gains = jnp.concatenate([plane.hop(gains, k) for k in range(rows)], axis=1).astype(F32)
    attn_gain_f, mlp_gain_f = gains[0:1], gains[1:2]
    q_gain_f = lax.dynamic_slice_in_dim(query_gain, row * head_part, head_part).astype(F32)
    k_gain_f = lax.dynamic_slice_in_dim(key_gain, row * head_part, head_part).astype(F32)

    def by_sequence(array):
        shape = (cols, rows, seq_own, tok_seq) + array.shape[1:]
        return jnp.swapaxes(array.reshape(shape), 1, 2).reshape(
            (seq_grp, seq_len) + array.shape[1:]
        )

    def by_block(array):
        shape = (cols, seq_own, rows, tok_seq) + array.shape[2:]
        return jnp.swapaxes(array.reshape(shape), 1, 2).reshape((tok_all,) + array.shape[2:])

    query_raw = dot(inputs_all, w_query)
    key_raw = dot(inputs_all, w_key)
    value_low = dot(inputs_all, w_value).astype(BF)
    squares = jnp.stack(
        [jnp.sum(query_raw * query_raw, axis=1), jnp.sum(key_raw * key_raw, axis=1)]
    )
    scales = lax.rsqrt(plane.total(squares) / width + EPSILON)
    q_scale = scales[0][:, None]
    k_scale = scales[1][:, None]
    block_rows = row ^ jnp.arange(rows, dtype=jnp.int32)
    places = (
        block_rows[:, None] * tok_seq + jnp.arange(tok_seq, dtype=jnp.int32)[None, :]
    ).reshape(seq_len)
    block_cols = col ^ jnp.arange(cols, dtype=jnp.int32)
    seq_ids = (
        my_group * seq_grp
        + block_cols[:, None] * seq_own
        + jnp.arange(seq_own, dtype=jnp.int32)[None, :]
    ).reshape(seq_grp)
    live_len = jnp.sum(
        jnp.where(
            seq_ids[:, None] == jnp.arange(seq_count, dtype=jnp.int32)[None, :], lengths[None, :], 0
        ),
        axis=1,
    )
    frequency = ROPE_THETA ** (-(jnp.arange(HD // 2).astype(F32) * 2.0 / HD))
    angles = places.astype(F32)[:, None] * frequency[None, :]
    cos_table = jnp.cos(angles)
    sin_table = jnp.sin(angles)
    cos_table = jnp.concatenate([cos_table, cos_table], axis=1)
    sin_table = jnp.concatenate([-sin_table, sin_table], axis=1)
    place_tables = places[:, None], places[None, :]

    def in_rows(array):
        return by_sequence(array).reshape(array.shape)

    def joined(array):
        return by_block(array.reshape(seq_grp, seq_len, head_part))

    values = in_rows(value_low)
    q_unit = query_raw * q_scale
    k_unit = key_raw * k_scale
    q_normed, k_normed = in_rows(q_unit * q_gain_f), in_rows(k_unit * k_gain_f)
    down_half = rows // 2
    out_pieces, down_pieces = together(out_pieces, down_pieces)
    down_pieces = [plane.hop(piece, k) for k, piece in enumerate(down_pieces)]
    up_far, q_normed = together(up_far, q_normed)
    down_pieces[: down_half + 1], values = together(down_pieces[: down_half + 1], values)
    w_out = jnp.concatenate(out_pieces, axis=1)
    up_far = over_groups(up_far)
    attn_mix, q_rot, k_rot = over_heads(
        attend_kernel, live_len, seq_len, (BF, BF, BF),
        q_normed, k_normed, values, cos_table, sin_table, *place_tables,
    )
    attn_mix = joined(attn_mix)
    up_far, down_pieces, attn_mix = together(up_far, down_pieces, attn_mix)
    attn_raw = plane.scatter(dot(attn_mix, w_out).astype(BF))
    w_gate = whole(gate_pieces, gate_far, 0)
    w_up = whole(up_pieces, up_far, 0)
    w_down = jnp.concatenate(down_pieces, axis=1)
    a_scale = rms_scale(attn_raw)
    a_unit = attn_raw * a_scale
    branch_a = a_unit * attn_gain_f
    hidden = inputs + branch_a
    hidden_all = plane.gather(hidden.astype(BF))
    gate_pre = dot(hidden_all, w_gate)
    up_pre = dot(hidden_all, w_up)
    gate_sig = jax.nn.sigmoid(gate_pre)
    gate_act = gate_pre * gate_sig
    inner_low = (gate_act * up_pre).astype(BF)
    mlp_raw = plane.scatter(dot(inner_low, w_down).astype(BF))
    m_scale = rms_scale(mlp_raw)
    m_unit = mlp_raw * m_scale
    branch_m = m_unit * mlp_gain_f
    result = (hidden + branch_m) * valid_rows

    d_m_unit = d_full * mlp_gain_f
    d_mlp = m_scale * (d_m_unit - m_unit * jnp.mean(d_m_unit * m_unit, axis=-1, keepdims=True))
    d_mlp_all = plane.gather(d_mlp.astype(BF))
    order = list(range(rows // 2, rows)) + list(range(rows // 2))
    near, far = slice(0, width // 2), slice(width // 2, width)
    low, high = slice(0, ff_part // 2), slice(ff_part // 2, ff_part)
    waiting = []

    def move(index, total):
        if index < 4:
            first = rows // 2 if index < 2 else 0
            blocks = jnp.split(total, rows // 2, axis=1)
            return [plane.hop(block, first + k) for k, block in enumerate(blocks)]
        if index == 4 + 2 * rows:
            return plane.hop(total[:part], order[0]), total[part:]
        return plane.hop(total, order[(index - 4) % rows])

    line = Line(move)

    def outer(left_side, right_side):
        return against(left_side, right_side).astype(BF)

    def step(values):
        return line.step(values, waiting.pop(0) if waiting else None)

    waiting += [outer(inner_low[:, low], d_mlp_all[:, far])]
    d_mlp_all = step(d_mlp_all)
    waiting += [outer(inner_low[:, high], d_mlp_all[:, far])]
    waiting += [outer(inner_low[:, half], d_mlp_all[:, near]) for half in (low, high)]
    d_inner = through(d_mlp_all, w_down)
    d_gate_low = (d_inner * up_pre * (gate_sig * (1.0 + gate_pre * (1.0 - gate_sig)))).astype(BF)
    d_up_low = (d_inner * gate_act).astype(BF)
    d_gate_low, d_up_low = step((d_gate_low, d_up_low))
    waiting += [outer(plane.slot(hidden_all, k), d_gate_low) for k in order]
    waiting += [outer(plane.slot(hidden_all, k), d_up_low) for k in order]
    partial = step((through(d_gate_low, w_gate) + through(d_up_low, w_up)).astype(BF))
    d_hidden = d_full + plane.scatter(partial, step)
    d_a_unit = d_hidden * attn_gain_f
    d_attn = a_scale * (d_a_unit - a_unit * jnp.mean(d_a_unit * a_unit, axis=-1, keepdims=True))
    d_attn_all = plane.gather(d_attn.astype(BF), step)
    d_mix = step(in_rows(through(d_attn_all, w_out).astype(BF)))
    d_qn, d_kn, d_value = over_heads(
        attend_back_kernel, live_len, seq_len, (F32, F32, BF),
        q_rot, k_rot, values, d_mix, cos_table, sin_table, *place_tables,
    )
    d_qn, d_kn, d_value = joined(d_qn), joined(d_kn), joined(d_value)
    d_q_hat = d_qn * q_gain_f
    d_k_hat = d_kn * k_gain_f
    d_q_hat, d_k_hat, d_value = step((d_q_hat, d_k_hat, d_value))
    inners = plane.total(
        jnp.stack([jnp.sum(d_q_hat * q_unit, axis=1), jnp.sum(d_k_hat * k_unit, axis=1)])
    )
    inners = step(inners)
    d_query = q_scale * (d_q_hat - q_unit * (inners[0] / width)[:, None])
    d_key = k_scale * (d_k_hat - k_unit * (inners[1] / width)[:, None])
    d_query = d_query.astype(BF)
    d_key = d_key.astype(BF)
    d_qkv = jnp.concatenate([d_query, d_key, d_value], axis=1)
    waiting += [
        jnp.concatenate(
            [
                outer(plane.slot(inputs_all, k), d_qkv),
                outer(plane.slot(d_attn_all, k), attn_mix),
            ],
            axis=1,
        )
        for k in order
    ]
    partial = step(
        (through(d_query, w_query) + through(d_key, w_key) + through(d_value, w_value)).astype(BF)
    )
    d_inputs = d_hidden + plane.scatter(partial)
    def sums_of(array):
        return jnp.sum(array.reshape(seq_own, tok_seq * width), axis=1)

    own_sums = jnp.stack(
        [
            sums_of(result * result),
            sums_of(branch_a * branch_a * valid_rows),
            sums_of(branch_m * branch_m * valid_rows),
        ],
        axis=1,
    )
    own_ids = my_group * seq_grp + first_own + jnp.arange(seq_own, dtype=jnp.int32)
    seq_sums = jnp.sum(
        jnp.where(
            own_ids[:, None, None] == jnp.arange(seq_count, dtype=jnp.int32)[None, :, None],
            own_sums[:, None, :],
            0.0,
        ),
        axis=0,
    )
    gain_sums = plane.relative(
        jnp.stack([jnp.sum(d_hidden * a_unit, axis=0), jnp.sum(d_full * m_unit, axis=0)])
    )
    head_sums = jnp.stack([jnp.sum(d_qn * q_unit, axis=0), jnp.sum(d_kn * k_unit, axis=0)])
    mine = (
        (jnp.arange(cols)[:, None] == col) & (jnp.arange(rows)[None, :] == row)
    ).astype(F32)
    head_sums = (head_sums[:, None, None, :] * mine[None, :, :, None]).reshape(2, cols, heads_cols)
    vector = jnp.concatenate([gain_sums.reshape(-1), head_sums.reshape(-1), seq_sums.reshape(-1)])
    vector = jnp.pad(vector, (0, -vector.shape[0] % (ff_part * 16))).reshape(-1, ff_part)
    row_xor = 1
    while row_xor < rows:
        vector = vector + plane.hop(vector, row_xor)
        row_xor *= 2
    col_xor = 1
    while col_xor < cols:
        vector = vector + plane.hop(vector, 0, col_xor)
        col_xor *= 2
    waiting[-rows] = jnp.concatenate([waiting[-rows], vector.astype(BF)], axis=0)
    while waiting:
        step(())
    line.placed, d_inputs, result_late = together(line.placed, d_inputs, result)

    def home(array):
        own = plane.relative((array).astype(BF)).reshape(seq_own, tok_seq, width)
        pieces = [own] + [plane.hop(own, 0, k) for k in range(1, cols)]
        out = jnp.zeros((seq_grp, tok_seq, width), BF)
        for k in range(cols):
            out = lax.dynamic_update_slice_in_dim(out, pieces[k], (col ^ k) * seq_own, axis=0)
        return out

    output = home(result_late)
    grad_input = home(d_inputs * valid_rows)

    def finish(blocks, axis):
        size = blocks[0].shape[axis]
        shape = list(blocks[0].shape)
        shape[axis] = size * rows
        out = jnp.zeros(shape, F32)
        for k in reversed(range(rows)):
            start = [0, 0]
            start[axis] = (row ^ k) * size
            out = lax.dynamic_update_slice(out, blocks[k].astype(F32), start)
        return out

    def arrived_at(placed):
        return [placed[order.index(k)] for k in range(rows)]

    placed = line.finish()
    placed[4 + 2 * rows], vector = placed[4 + 2 * rows]
    vector = vector.astype(F32).reshape(-1)
    grad_down = [placed[2] + placed[0], placed[3] + placed[1]]
    grad_down = finish([jnp.concatenate(both, axis=0) for both in zip(*grad_down, strict=True)], 0)
    grad_gate = finish(arrived_at(placed[4 : 4 + rows]), 1)
    grad_up = finish(arrived_at(placed[4 + rows : 4 + 2 * rows]), 1)
    attn_blocks = arrived_at(placed[4 + 2 * rows :])
    grad_query, grad_key, grad_value, grad_out = (
        [block[:, k * head_part : (k + 1) * head_part] for block in attn_blocks] for k in range(4)
    )
    grad_query, grad_key, grad_value = (
        finish(blocks, 1) for blocks in (grad_query, grad_key, grad_value)
    )
    grad_out = finish([block.T for block in grad_out], 0)

    gain_sums = lax.dynamic_slice_in_dim(
        vector[: 2 * width].reshape(2, width), row * part, part, axis=1
    )
    head_end = 2 * width + 2 * cols * heads_cols
    head_sums = lax.dynamic_slice_in_dim(
        vector[2 * width : head_end].reshape(2, cols, heads_cols), col, 1, axis=1
    )
    seq_sums = vector[head_end : head_end + 3 * seq_count].reshape(seq_count, 3)
    member = (
        (deal_slot // seq_grp)[:, None] == jnp.arange(groups, dtype=jnp.int32)[None, :]
    ).astype(F32)
    counts = jnp.sum(member * lengths.astype(F32)[:, None], axis=0)
    stat_sums = jnp.sum(member[:, :, None] * seq_sums[:, None, :], axis=0)
    rms_stats = jnp.sqrt(stat_sums / (counts[:, None] * width))
    return (
        output,
        grad_input,
        grad_query,
        grad_key,
        grad_value,
        grad_out,
        head_sums[0, 0],
        head_sums[1, 0],
        gain_sums[0],
        grad_gate,
        grad_up,
        grad_down,
        gain_sums[1],
        rms_stats,
    )


def solution(mesh):
    tokens = P("dp", "row", None)
    inward = P("row", "col")
    outward = P("col", "row")
    in_specs = (
        (tokens, tokens, P(), P())
        + (inward, inward, inward, outward)
        + (P("col"), P("col"), P("row"))
        + (inward, inward, outward, P("row"))
    )
    out_specs = (
        (tokens, tokens)
        + (inward, inward, inward, outward)
        + (P("col"), P("col"), P("row"))
        + (inward, inward, outward, P("row"))
        + (P(),)
    )
    return jax.shard_map(shards, mesh=mesh, in_specs=in_specs, out_specs=out_specs, check_vma=False)
```

```python
import jax
import jax.numpy as jnp
from jax import lax
from jax.experimental import pallas as pl
from jax.experimental.pallas import tpu as pltpu
from jax.sharding import PartitionSpec as P

HD = 128
EPSILON = 1e-06
ROPE_THETA = 500000.0
MASK_VALUE = 1e30
BF = jnp.bfloat16
F32 = jnp.float32


def rms_scale(matrix):
    return lax.rsqrt(jnp.mean(matrix * matrix, axis=-1, keepdims=True) + EPSILON)


def masked_prob(length, q_rot, k_rot, place_col, place_row):
    scores = through(q_rot, k_rot) * HD ** (-0.5)
    allowed = (place_row <= place_col) & (place_row < length)
    scores = jnp.where(allowed, scores, -MASK_VALUE)
    exponent = jnp.exp(scores - jnp.max(scores, axis=-1, keepdims=True))
    return exponent / jnp.sum(exponent, axis=-1, keepdims=True)


def attend_kernel(
    length, query, key, value, cos, sin, place_col, place_row, mix, q_out, k_out
):
    def turned(normed):
        normed = normed[...]
        return (normed * cos[...] + pltpu.roll(normed, HD // 2, 1) * sin[...]).astype(BF)

    q_rot, k_rot = turned(query), turned(key)
    q_out[...], k_out[...] = q_rot, k_rot
    prob = masked_prob(length[pl.program_id(0)], q_rot, k_rot, place_col[...], place_row[...])
    mix[...] = dot(prob.astype(BF), value[...]).astype(BF)


def attend_back_kernel(
    length, q_rot, k_rot, value, d_mix, cos, sin, place_col, place_row, d_query, d_key, d_value
):
    q_rot, k_rot, d_mix = q_rot[...], k_rot[...], d_mix[...]
    prob = masked_prob(length[pl.program_id(0)], q_rot, k_rot, place_col[...], place_row[...])
    d_value[...] = against(prob.astype(BF), d_mix).astype(BF)
    d_prob = through(d_mix, value[...])
    row_delta = jnp.sum(prob * d_prob, axis=-1, keepdims=True)
    d_scores = (prob * (d_prob - row_delta)).astype(BF)

    def turned_back(grad):
        grad = grad * HD ** (-0.5)
        return grad * cos[...] - pltpu.roll(grad, HD // 2, 1) * sin[...]

    d_query[...] = turned_back(dot(d_scores, k_rot))
    d_key[...] = turned_back(against(d_scores, q_rot))


def over_heads(kernel, lengths, seq_len, outs, *arrays):
    tokens, features = arrays[0].shape

    def spec(shape):
        if shape == (tokens, features):
            return pl.BlockSpec((seq_len, HD), lambda s, h, *_: (s, h))
        return pl.BlockSpec(shape, lambda s, h, *_: (0, 0))

    count = tokens * features // HD
    return pl.pallas_call(
        kernel,
        out_shape=tuple(jax.ShapeDtypeStruct((tokens, features), dtype) for dtype in outs),
        grid_spec=pltpu.PrefetchScalarGridSpec(
            num_scalar_prefetch=1,
            grid=(tokens // seq_len, features // HD),
            in_specs=[spec(array.shape) for array in arrays],
            out_specs=tuple(spec((tokens, features)) for _ in outs),
        ),
        cost_estimate=pl.CostEstimate(
            flops=4 * len(outs) * count * seq_len * HD,
            bytes_accessed=4 * (len(arrays) + len(outs)) * tokens * features,
            transcendentals=count * seq_len,
        ),
    )(lengths, *arrays)


def dot(left_side, right_side):
    return jnp.dot(left_side, right_side, preferred_element_type=F32)


def against(left_side, right_side):
    return lax.dot_general(
        left_side, right_side, (((0,), (0,)), ((), ())), preferred_element_type=F32
    )


def through(left_side, weight):
    return lax.dot_general(
        left_side, weight, (((1,), (1,)), ((), ())), preferred_element_type=F32
    )


def together(*values):
    return lax.optimization_barrier(values)


def unchanged(value):
    return value


class Plane:
    def __init__(self, width):
        self.rows = lax.axis_size("row")
        self.cols = lax.axis_size("col")
        self.row = lax.axis_index("row")
        self.col = lax.axis_index("col")
        self.part = width // self.rows

    def hop(self, array, row_xor, col_xor=0):
        if row_xor and col_xor:
            pairs = [
                (a * self.cols + b, (a ^ row_xor) * self.cols + (b ^ col_xor))
                for a in range(self.rows)
                for b in range(self.cols)
            ]
            return lax.ppermute(array, ("row", "col"), pairs)
        if row_xor:
            return lax.ppermute(array, "row", [(a, a ^ row_xor) for a in range(self.rows)])
        if col_xor:
            return lax.ppermute(array, "col", [(a, a ^ col_xor) for a in range(self.cols)])
        return array

    def slot(self, array, index):
        return array[..., index * self.part : (index + 1) * self.part]

    def turn(self, array, row_xor):
        if row_xor == 0:
            return array
        return jnp.concatenate(
            [self.slot(array, index ^ row_xor) for index in range(self.rows)], axis=-1
        )

    def relative(self, array):
        return jnp.concatenate(
            [
                lax.dynamic_slice_in_dim(
                    array, (self.row ^ index) * self.part, self.part, axis=array.ndim - 1
                )
                for index in range(self.rows)
            ],
            axis=-1,
        )

    def gather(self, own, step=unchanged):
        blocks = {(0, 0): own}
        if self.rows == 4 and self.cols == 2:
            half = own.shape[0] // 2
            blocks[0, 2] = self.hop(self.turn(own, 2), 2)
            blocks[1, 0] = self.hop(own, 0, 1)
            blocks = step(blocks)
            blocks[1, 2] = jnp.concatenate(
                [
                    self.hop(blocks[0, 2][:half], 0, 1),
                    self.hop(self.turn(blocks[1, 0][half:], 2), 2),
                ],
                axis=0,
            )
        else:
            for col_xor in reversed(range(self.cols)):
                for row_xor in reversed(range(0, self.rows, 2)):
                    blocks[col_xor, row_xor] = self.hop(self.turn(own, row_xor), row_xor, col_xor)
        return step(self.over_cores(blocks))

    def over_cores(self, blocks):
        for col_xor in range(self.cols):
            for row_xor in range(0, self.rows, 2):
                blocks[col_xor, row_xor + 1] = self.hop(
                    self.turn(blocks[col_xor, row_xor], 1), 1
                )
        return jnp.concatenate(
            [blocks[b, a] for b in range(self.cols) for a in range(self.rows)], axis=0
        )

    def gather_columns(self, own):
        blocks = {}
        for row_xor in range(0, self.rows, 2):
            arrived = self.hop(self.turn(own[0], row_xor), row_xor)
            for col_xor in range(self.cols):
                if row_xor:
                    blocks[col_xor, row_xor] = self.hop(arrived, 0, col_xor)
                else:
                    blocks[col_xor, row_xor] = own[col_xor]
        return self.over_cores(blocks)

    def scatter(self, partial, step=unchanged):
        tokens = partial.shape[0] // (self.rows * self.cols)
        blocks = partial.reshape(self.cols, self.rows, tokens, -1)
        if self.rows == 4 and self.cols == 2:
            half = tokens // 2
            away = self.hop(self.turn(jnp.stack([blocks[:, 1], blocks[:, 3]]), 1), 1)
            away, blocks = step((away, blocks))
            near = [blocks[:, 2 * k].astype(F32) + away[k].astype(F32) for k in range(2)]
            by_row = self.hop(self.turn(near[1][:, :half].astype(BF), 2), 2)
            far = jnp.stack([near[0][1, half:], near[1][1, half:]]).astype(BF)
            by_col = self.hop(far, 0, 1)
            by_row, by_col, near = step((by_row, by_col, near))
            first = [near[0][k, :half] + by_row[k].astype(F32) for k in range(2)]
            second = [near[k][0, half:] + by_col[k].astype(F32) for k in range(2)]
            last_col = self.hop(first[1].astype(BF), 0, 1).astype(F32)
            last_row = self.hop(self.turn(second[1].astype(BF), 2), 2).astype(F32)
            return step(jnp.concatenate([first[0] + last_col, second[0] + last_row], axis=0))
        sums = {}
        for col_xor in reversed(range(self.cols)):
            for row_xor in reversed(range(0, self.rows, 2)):
                arrived = self.hop(self.turn(blocks[col_xor, row_xor + 1], 1), 1)
                sums[col_xor, row_xor] = blocks[col_xor, row_xor].astype(F32) + arrived.astype(F32)
        total = sums[0, 0]
        for col_xor in reversed(range(self.cols)):
            for row_xor in reversed(range(0, self.rows, 2)):
                if col_xor or row_xor:
                    sent = self.turn(sums[col_xor, row_xor].astype(BF), row_xor)
                    total = total + self.hop(sent, row_xor, col_xor).astype(F32)
        return total

    def total(self, array):
        blocks = array.reshape(array.shape[:-1] + (self.cols, self.rows, -1))
        row_xor = 1
        while row_xor < self.rows:
            order = [index ^ row_xor for index in range(self.rows)]
            arrived = self.hop(blocks, row_xor)
            blocks = blocks + jnp.stack([arrived[..., k, :] for k in order], axis=-2)
            row_xor *= 2
        col_xor = 1
        while col_xor < self.cols:
            order = [index ^ col_xor for index in range(self.cols)]
            arrived = self.hop(blocks, 0, col_xor)
            blocks = blocks + jnp.stack([arrived[..., k, :, :] for k in order], axis=-3)
            col_xor *= 2
        return blocks.reshape(array.shape)


ENDS = [(0, 1), (1, 0), (2, 3), (3, 2)]
MIDDLE = [(1, 2), (2, 1)]


def plus(one, other):
    return (one.astype(F32) + other.astype(F32)).astype(BF)


class Line:
    depth = 2

    def __init__(self, move):
        self.move = move
        self.line = lax.axis_size("dp") == 4
        place = lax.axis_index("dp")
        self.inner = (place == 1) | (place == 2)
        self.arrays, self.pairs, self.full, self.placed = [], [], [], []
        self.pending = [{}] * self.depth
        self.moving = [[]] * (self.depth + 1)
        self.sent_back = 0

    def step(self, values, array=None):
        if not self.line:
            if array is not None:
                self.arrays.append(array)
            return values
        if 0 < len(self.arrays) <= self.depth + 2:
            last = self.pending[-1]
            last["inward"], array = together(last["inward"], array)
        pending, moving, array, values = together(
            self.pending.pop(0), self.moving.pop(0), array, values
        )
        self.advance(pending, moving, array)
        return values

    def advance(self, pending, moving, array):
        self.placed += moving
        current, moved = {}, []
        if "back" in pending:
            total = jnp.where(self.inner, pending["full"], pending["back"])
            moved.append(self.move(len(self.placed) + sum(map(len, self.moving)), total))
        self.moving.append(moved)
        if "across" in pending:
            self.full.append(plus(self.pairs[len(self.full)], pending["across"]))
        if "inward" in pending:
            pair = plus(self.arrays[len(self.pairs)], pending["inward"])
            self.pairs.append(pair)
            current["across"] = lax.ppermute(pair, "dp", MIDDLE)
        back = None
        if len(self.full) > self.sent_back:
            back = self.full[self.sent_back]
            self.sent_back += 1
        if array is not None:
            self.arrays.append(array)
        if back is not None and array is not None and back.shape == array.shape:
            sent = jnp.where(self.inner, back, array)
            current["full"] = sent
            current["inward"] = lax.ppermute(sent, "dp", ENDS)
            current["back"] = current["inward"]
        else:
            if array is not None:
                current["inward"] = lax.ppermute(array, "dp", [(0, 1), (3, 2)])
            if back is not None:
                current["full"] = back
                current["back"] = lax.ppermute(back, "dp", [(1, 0), (2, 3)])
        self.pending.append(current)

    def finish(self):
        if not self.line:
            totals = [lax.psum(array, "dp") for array in self.arrays]
            return [self.move(index, total) for index, total in enumerate(totals)]
        while len(self.placed) < len(self.arrays):
            self.advance(self.pending.pop(0), self.moving.pop(0), None)
        return self.placed


def shards(
    layer_input,
    cotangent,
    lengths,
    deal_slot,
    query_weight,
    key_weight,
    value_weight,
    out_weight,
    query_gain,
    key_gain,
    attn_gain,
    gate_weight,
    up_weight,
    down_weight,
    mlp_gain,
):
    groups = lax.axis_size("dp")
    my_group = lax.axis_index("dp")
    seq_grp, tok_seq, width = layer_input.shape
    seq_count = lengths.shape[0]
    plane = Plane(width)
    rows, cols, row, col, part = plane.rows, plane.cols, plane.row, plane.col, plane.part
    seq_own = seq_grp // cols
    tok_own = seq_own * tok_seq
    seq_len = tok_seq * rows
    tok_all = seq_grp * seq_len
    heads_cols = query_weight.shape[1]
    head_part = heads_cols // rows
    ff_part = gate_weight.shape[1] // rows

    first_own = col * seq_own
    all_input = plane.relative(layer_input)
    own_cot = plane.relative(
        lax.dynamic_slice_in_dim(cotangent, first_own, seq_own, axis=0).reshape(tok_own, width)
    )
    own_places = row * tok_seq + jnp.arange(tok_seq, dtype=jnp.int32)
    group_len = lax.dynamic_slice_in_dim(lengths, my_group * seq_grp, seq_grp)
    valid_all = (own_places[None, :] < group_len[:, None]).astype(BF)
    all_input = (all_input * valid_all[:, :, None]).reshape(cols, tok_own, width)
    all_input = jnp.stack(
        [
            lax.dynamic_index_in_dim(all_input, col ^ index, axis=0, keepdims=False)
            for index in range(cols)
        ]
    )
    inputs_low = all_input[0]
    own_len = lax.dynamic_slice_in_dim(lengths, my_group * seq_grp + first_own, seq_own)
    valid_rows = (own_places[None, :] < own_len[:, None]).astype(F32).reshape(tok_own, 1)
    inputs = inputs_low.astype(F32)
    d_full = own_cot.astype(F32) * valid_rows
    inputs_all = plane.gather_columns(all_input)

    def pieces_of(weight, axis):
        size = weight.shape[axis] // rows
        return [
            lax.dynamic_slice_in_dim(weight, (row ^ k) * size, size, axis=axis)
            for k in range(rows)
        ]

    def shared(weight, axis):
        pieces = pieces_of(weight, axis)
        size = pieces[0].shape[0] // groups
        parts = [
            plane.hop(lax.dynamic_slice_in_dim(piece, my_group * size, size, axis=0), k)
            for k, piece in enumerate(pieces)
            if k >= 2
        ]
        return pieces[:1] + [plane.hop(pieces[1], 1)], jnp.concatenate(parts, axis=1)

    def whole(pieces, far, axis):
        return jnp.concatenate(pieces + jnp.split(far, rows - 2, axis=1), axis=axis)

    def over_groups(part):
        return lax.all_gather(part, "dp", axis=0, tiled=True)

    gate_pieces, gate_far = shared(gate_weight, 1)
    trios = [
        jnp.stack(trio)
        for trio in zip(
            pieces_of(query_weight, 1),
            pieces_of(key_weight, 1),
            pieces_of(value_weight, 1),
            strict=True,
        )
    ]
    gate_far, trios[2:] = together(gate_far, trios[2:])
    gate_far = over_groups(gate_far)
    trios = [plane.hop(trio, k) for k, trio in enumerate(trios)]
    gate_far, trios, inputs_all = together(gate_far, trios, inputs_all)
    up_pieces, up_far = shared(up_weight, 1)
    down_pieces = pieces_of(down_weight, 0)
    w_query, w_key, w_value = (
        jnp.concatenate([trio[k] for trio in trios], axis=0) for k in range(3)
    )
    out_pieces = [plane.hop(piece, k) for k, piece in enumerate(pieces_of(out_weight, 0))]
    gains = jnp.stack([attn_gain, mlp_gain])
    gains = jnp.concatenate([plane.hop(gains, k) for k in range(rows)], axis=1).astype(F32)
    attn_gain_f, mlp_gain_f = gains[0:1], gains[1:2]
    q_gain_f = lax.dynamic_slice_in_dim(query_gain, row * head_part, head_part).astype(F32)
    k_gain_f = lax.dynamic_slice_in_dim(key_gain, row * head_part, head_part).astype(F32)

    def by_sequence(array):
        shape = (cols, rows, seq_own, tok_seq) + array.shape[1:]
        return jnp.swapaxes(array.reshape(shape), 1, 2).reshape(
            (seq_grp, seq_len) + array.shape[1:]
        )

    def by_block(array):
        shape = (cols, seq_own, rows, tok_seq) + array.shape[2:]
        return jnp.swapaxes(array.reshape(shape), 1, 2).reshape((tok_all,) + array.shape[2:])

    query_raw = dot(inputs_all, w_query)
    key_raw = dot(inputs_all, w_key)
    value_low = dot(inputs_all, w_value).astype(BF)
    squares = jnp.stack(
        [jnp.sum(query_raw * query_raw, axis=1), jnp.sum(key_raw * key_raw, axis=1)]
    )
    scales = lax.rsqrt(plane.total(squares) / width + EPSILON)
    q_scale = scales[0][:, None]
    k_scale = scales[1][:, None]
    block_rows = row ^ jnp.arange(rows, dtype=jnp.int32)
    places = (
        block_rows[:, None] * tok_seq + jnp.arange(tok_seq, dtype=jnp.int32)[None, :]
    ).reshape(seq_len)
    block_cols = col ^ jnp.arange(cols, dtype=jnp.int32)
    seq_ids = (
        my_group * seq_grp
        + block_cols[:, None] * seq_own
        + jnp.arange(seq_own, dtype=jnp.int32)[None, :]
    ).reshape(seq_grp)
    live_len = jnp.sum(
        jnp.where(
            seq_ids[:, None] == jnp.arange(seq_count, dtype=jnp.int32)[None, :], lengths[None, :], 0
        ),
        axis=1,
    )
    frequency = ROPE_THETA ** (-(jnp.arange(HD // 2).astype(F32) * 2.0 / HD))
    angles = places.astype(F32)[:, None] * frequency[None, :]
    cos_table = jnp.cos(angles)
    sin_table = jnp.sin(angles)
    cos_table = jnp.concatenate([cos_table, cos_table], axis=1)
    sin_table = jnp.concatenate([-sin_table, sin_table], axis=1)
    place_tables = places[:, None], places[None, :]

    def in_rows(array):
        return by_sequence(array).reshape(array.shape)

    def joined(array):
        return by_block(array.reshape(seq_grp, seq_len, head_part))

    values = in_rows(value_low)
    q_unit = query_raw * q_scale
    k_unit = key_raw * k_scale
    q_normed, k_normed = in_rows(q_unit * q_gain_f), in_rows(k_unit * k_gain_f)
    down_half = rows // 2
    out_pieces, down_pieces = together(out_pieces, down_pieces)
    down_pieces = [plane.hop(piece, k) for k, piece in enumerate(down_pieces)]
    up_far, q_normed = together(up_far, q_normed)
    down_pieces[: down_half + 1], values = together(down_pieces[: down_half + 1], values)
    w_out = jnp.concatenate(out_pieces, axis=1)
    up_far = over_groups(up_far)
    attn_mix, q_rot, k_rot = over_heads(
        attend_kernel, live_len, seq_len, (BF, BF, BF),
        q_normed, k_normed, values, cos_table, sin_table, *place_tables,
    )
    attn_mix = joined(attn_mix)
    up_far, down_pieces, attn_mix = together(up_far, down_pieces, attn_mix)
    attn_raw = plane.scatter(dot(attn_mix, w_out).astype(BF))
    w_gate = whole(gate_pieces, gate_far, 0)
    w_up = whole(up_pieces, up_far, 0)
    w_down = jnp.concatenate(down_pieces, axis=1)
    a_scale = rms_scale(attn_raw)
    a_unit = attn_raw * a_scale
    branch_a = a_unit * attn_gain_f
    hidden = inputs + branch_a
    hidden_all = plane.gather(hidden.astype(BF))
    gate_pre = dot(hidden_all, w_gate)
    up_pre = dot(hidden_all, w_up)
    gate_sig = jax.nn.sigmoid(gate_pre)
    gate_act = gate_pre * gate_sig
    inner_low = (gate_act * up_pre).astype(BF)
    mlp_raw = plane.scatter(dot(inner_low, w_down).astype(BF))
    m_scale = rms_scale(mlp_raw)
    m_unit = mlp_raw * m_scale
    branch_m = m_unit * mlp_gain_f
    result = (hidden + branch_m) * valid_rows

    d_m_unit = d_full * mlp_gain_f
    d_mlp = m_scale * (d_m_unit - m_unit * jnp.mean(d_m_unit * m_unit, axis=-1, keepdims=True))
    d_mlp_all = plane.gather(d_mlp.astype(BF))
    order = list(range(rows // 2, rows)) + list(range(rows // 2))
    near, far = slice(0, width // 2), slice(width // 2, width)
    low, high = slice(0, ff_part // 2), slice(ff_part // 2, ff_part)
    waiting = []

    def move(index, total):
        if index < 4:
            first = rows // 2 if index < 2 else 0
            blocks = jnp.split(total, rows // 2, axis=1)
            return [plane.hop(block, first + k) for k, block in enumerate(blocks)]
        if index == 4 + 2 * rows:
            return plane.hop(total[:part], order[0]), total[part:]
        return plane.hop(total, order[(index - 4) % rows])

    line = Line(move)

    def outer(left_side, right_side):
        return against(left_side, right_side).astype(BF)

    def step(values):
        return line.step(values, waiting.pop(0) if waiting else None)

    waiting += [outer(inner_low[:, low], d_mlp_all[:, far])]
    d_mlp_all = step(d_mlp_all)
    waiting += [outer(inner_low[:, high], d_mlp_all[:, far])]
    waiting += [outer(inner_low[:, half], d_mlp_all[:, near]) for half in (low, high)]
    d_inner = through(d_mlp_all, w_down)
    d_gate_low = (d_inner * up_pre * (gate_sig * (1.0 + gate_pre * (1.0 - gate_sig)))).astype(BF)
    d_up_low = (d_inner * gate_act).astype(BF)
    d_gate_low, d_up_low = step((d_gate_low, d_up_low))
    waiting += [outer(plane.slot(hidden_all, k), d_gate_low) for k in order]
    waiting += [outer(plane.slot(hidden_all, k), d_up_low) for k in order]
    partial = step((through(d_gate_low, w_gate) + through(d_up_low, w_up)).astype(BF))
    d_hidden = d_full + plane.scatter(partial, step)
    d_a_unit = d_hidden * attn_gain_f
    d_attn = a_scale * (d_a_unit - a_unit * jnp.mean(d_a_unit * a_unit, axis=-1, keepdims=True))
    d_attn_all = plane.gather(d_attn.astype(BF), step)
    d_mix = step(in_rows(through(d_attn_all, w_out).astype(BF)))
    d_qn, d_kn, d_value = over_heads(
        attend_back_kernel, live_len, seq_len, (F32, F32, BF),
        q_rot, k_rot, values, d_mix, cos_table, sin_table, *place_tables,
    )
    d_qn, d_kn, d_value = joined(d_qn), joined(d_kn), joined(d_value)
    d_q_hat = d_qn * q_gain_f
    d_k_hat = d_kn * k_gain_f
    d_q_hat, d_k_hat, d_value = step((d_q_hat, d_k_hat, d_value))
    inners = plane.total(
        jnp.stack([jnp.sum(d_q_hat * q_unit, axis=1), jnp.sum(d_k_hat * k_unit, axis=1)])
    )
    inners = step(inners)
    d_query = q_scale * (d_q_hat - q_unit * (inners[0] / width)[:, None])
    d_key = k_scale * (d_k_hat - k_unit * (inners[1] / width)[:, None])
    d_query = d_query.astype(BF)
    d_key = d_key.astype(BF)
    d_qkv = jnp.concatenate([d_query, d_key, d_value], axis=1)
    waiting += [
        jnp.concatenate(
            [
                outer(plane.slot(inputs_all, k), d_qkv),
                outer(plane.slot(d_attn_all, k), attn_mix),
            ],
            axis=1,
        )
        for k in order
    ]
    partial = step(
        (through(d_query, w_query) + through(d_key, w_key) + through(d_value, w_value)).astype(BF)
    )
    def sums_of(array):
        return jnp.sum(array.reshape(seq_own, tok_seq * width), axis=1)

    own_sums = jnp.stack(
        [
            sums_of(result * result),
            sums_of(branch_a * branch_a * valid_rows),
            sums_of(branch_m * branch_m * valid_rows),
        ],
        axis=1,
    )
    own_ids = my_group * seq_grp + first_own + jnp.arange(seq_own, dtype=jnp.int32)
    seq_sums = jnp.sum(
        jnp.where(
            own_ids[:, None, None] == jnp.arange(seq_count, dtype=jnp.int32)[None, :, None],
            own_sums[:, None, :],
            0.0,
        ),
        axis=0,
    )
    gain_sums = plane.relative(
        jnp.stack([jnp.sum(d_hidden * a_unit, axis=0), jnp.sum(d_full * m_unit, axis=0)])
    )
    head_sums = jnp.stack([jnp.sum(d_qn * q_unit, axis=0), jnp.sum(d_kn * k_unit, axis=0)])
    mine = (
        (jnp.arange(cols)[:, None] == col) & (jnp.arange(rows)[None, :] == row)
    ).astype(F32)
    head_sums = (head_sums[:, None, None, :] * mine[None, :, :, None]).reshape(2, cols, heads_cols)
    vector = jnp.concatenate([gain_sums.reshape(-1), head_sums.reshape(-1), seq_sums.reshape(-1)])
    vector = jnp.pad(vector, (0, -vector.shape[0] % (ff_part * 16))).reshape(-1, ff_part)
    row_xor = 1
    while row_xor < rows:
        vector = vector + plane.hop(vector, row_xor)
        row_xor *= 2
    col_xor = 1
    while col_xor < cols:
        vector = vector + plane.hop(vector, 0, col_xor)
        col_xor *= 2
    waiting[-rows] = jnp.concatenate([waiting[-rows], vector.astype(BF)], axis=0)
    while len(waiting) > 1:
        step(())
    partial = step(partial)
    d_inputs = d_hidden + plane.scatter(partial)
    d_inputs, result_late = together(d_inputs, result)

    def home(array):
        own = plane.relative((array).astype(BF)).reshape(seq_own, tok_seq, width)
        pieces = [own] + [plane.hop(own, 0, k) for k in range(1, cols)]
        out = jnp.zeros((seq_grp, tok_seq, width), BF)
        for k in range(cols):
            out = lax.dynamic_update_slice_in_dim(out, pieces[k], (col ^ k) * seq_own, axis=0)
        return out

    output = home(result_late)
    grad_input = home(d_inputs * valid_rows)

    def finish(blocks, axis):
        size = blocks[0].shape[axis]
        shape = list(blocks[0].shape)
        shape[axis] = size * rows
        out = jnp.zeros(shape, F32)
        for k in reversed(range(rows)):
            start = [0, 0]
            start[axis] = (row ^ k) * size
            out = lax.dynamic_update_slice(out, blocks[k].astype(F32), start)
        return out

    def arrived_at(placed):
        return [placed[order.index(k)] for k in range(rows)]

    placed = line.finish()
    placed[4 + 2 * rows], vector = placed[4 + 2 * rows]
    vector = vector.astype(F32).reshape(-1)
    grad_down = [placed[2] + placed[0], placed[3] + placed[1]]
    grad_down = finish([jnp.concatenate(both, axis=0) for both in zip(*grad_down, strict=True)], 0)
    grad_gate = finish(arrived_at(placed[4 : 4 + rows]), 1)
    grad_up = finish(arrived_at(placed[4 + rows : 4 + 2 * rows]), 1)
    attn_blocks = arrived_at(placed[4 + 2 * rows :])
    grad_query, grad_key, grad_value, grad_out = (
        [block[:, k * head_part : (k + 1) * head_part] for block in attn_blocks] for k in range(4)
    )
    grad_query, grad_key, grad_value = (
        finish(blocks, 1) for blocks in (grad_query, grad_key, grad_value)
    )
    grad_out = finish([block.T for block in grad_out], 0)

    gain_sums = lax.dynamic_slice_in_dim(
        vector[: 2 * width].reshape(2, width), row * part, part, axis=1
    )
    head_end = 2 * width + 2 * cols * heads_cols
    head_sums = lax.dynamic_slice_in_dim(
        vector[2 * width : head_end].reshape(2, cols, heads_cols), col, 1, axis=1
    )
    seq_sums = vector[head_end : head_end + 3 * seq_count].reshape(seq_count, 3)
    member = (
        (deal_slot // seq_grp)[:, None] == jnp.arange(groups, dtype=jnp.int32)[None, :]
    ).astype(F32)
    counts = jnp.sum(member * lengths.astype(F32)[:, None], axis=0)
    stat_sums = jnp.sum(member[:, :, None] * seq_sums[:, None, :], axis=0)
    rms_stats = jnp.sqrt(stat_sums / (counts[:, None] * width))
    return (
        output,
        grad_input,
        grad_query,
        grad_key,
        grad_value,
        grad_out,
        head_sums[0, 0],
        head_sums[1, 0],
        gain_sums[0],
        grad_gate,
        grad_up,
        grad_down,
        gain_sums[1],
        rms_stats,
    )


def solution(mesh):
    tokens = P("dp", "row", None)
    inward = P("row", "col")
    outward = P("col", "row")
    in_specs = (
        (tokens, tokens, P(), P())
        + (inward, inward, inward, outward)
        + (P("col"), P("col"), P("row"))
        + (inward, inward, outward, P("row"))
    )
    out_specs = (
        (tokens, tokens)
        + (inward, inward, inward, outward)
        + (P("col"), P("col"), P("row"))
        + (inward, inward, outward, P("row"))
        + (P(),)
    )
    return jax.shard_map(shards, mesh=mesh, in_specs=in_specs, out_specs=out_specs, check_vma=False)
```
